32 devices in a mesh: band: 4 (over x, core), mem: 8 (over z, y).
Axes of the slice: x: 2, y: 2, z: 4, core: 2. Of those that a mesh axis runs over, the one named last changes fastest.
Arguments:
- members: bfloat16 [64, 16, 8192], P('band', None, 'mem'), may hold values from -6 to 6
- eigvecs: bfloat16 [112, 16, 8192], P('band', None, 'mem'), may hold values from -6 to 6
- control: float32 [112, 64], replicated, may hold values from -6 to 6
- columns: int32 [512, 16], P('mem'), may hold values from 0 to 1023
- interpolation: bfloat16 [512, 256, 512], P('mem'), may hold values from -0.375 to 0.375
- owners: int32 [512], replicated, may hold values from 0 to 7, as said below
- innovation: float32 [8, 256, 512], P('mem'), may hold values from -6 to 6
- obs_weight: float32 [8, 256, 512], P('mem'), may hold values from 0.25 to 4
Outputs:
- gradient: float32 [112, 64], P(None, 'band')
- departures: float32 [8, 256, 512], P('mem', None, 'band')
The draws below stay inside these ranges and needn't reach their ends.
Inputs may be any that keep to these rules, and one draw needn't show every extreme that they name: `owners`: one tile sends at most 32 of its blocks to one owner, and some owner holds exactly 32 blocks from every tile.
All inputs are finite; a program needn't handle non-finite values.
Results may differ from the reference program's by a relative error of at most 0.0032.
Values may be sent and summed in bfloat16 or wider, within the bound.
A program may use at most 64 MiB of HBM per device.

```python
import math
import jax
import jax.numpy as jnp
from jax import lax

MEMBERS = 64
MODES = 112
LEVELS = 16
PATCH = 16
OBS_BLOCK = 512
TILE_COLS = 1024
BLOCKS = 64
TILES = 8
GRID = 8192
CAPACITY = 32
SLOTS = 256


def draw_owners(key, part):
    base_key = jax.random.fold_in(key, 11)
    hot_key, shift_key, order_key = jax.random.split(base_key, 3)
    hottest = jax.random.randint(hot_key, (), 0, TILES)
    shifts = jax.random.randint(shift_key, (TILES,), 0, TILES - 1)
    places = jnp.arange(BLOCKS, dtype=jnp.int32)
    others = (places[None, :] - CAPACITY + shifts[:, None]) % (TILES - 1)
    chosen = jnp.where(places[None, :] < CAPACITY, hottest, (hottest + 1 + others) % TILES)
    tile_keys = jax.random.split(order_key, TILES)
    orders = jax.vmap(lambda k: jax.random.permutation(k, BLOCKS))(tile_keys)
    shuffled = jnp.take_along_axis(chosen, orders, axis=1)
    return shuffled.reshape(-1).astype(jnp.int32)


def plant(values, key, smallest, largest):
    place = [jax.random.randint(jax.random.fold_in(key, axis), (), 0, length) for axis, length in enumerate(values.shape)]
    main_axis = values.shape.index(max(values.shape))
    beside = place[:main_axis] + [(place[main_axis] + 1) % values.shape[main_axis]] + place[main_axis + 1:]
    return values.at[tuple(place)].set(smallest).at[tuple(beside)].set(largest)


def levels(key, dims, shards, least, top_value):
    def one(dim, blocks):
        heights = jax.random.uniform(jax.random.fold_in(jax.random.fold_in(key, 6), dim), (blocks,), jnp.float32, least / len(shards), top_value / len(shards))
        return jnp.repeat(jnp.exp(heights), dims[dim] // blocks).reshape((-1,) + (1,) * (len(dims) - dim - 1))

    level = one(*shards[0])
    for cut in shards[1:]:
        level = level * one(*cut)
    return level


def scatter_about(own_key, dims, deviation, reach, cuts=(), kind=jnp.bfloat16):
    loudness = levels(own_key, dims, cuts, -0.22, 0.18) if cuts else 1.0
    values = jax.random.normal(own_key, dims, jnp.float32) * deviation * loudness
    return jnp.minimum(jnp.maximum(values, -reach), reach).astype(kind)


def setup_inputs(seed: int = 0) -> dict:
    seeds = jax.random.split(jax.random.key(seed), 9)
    members = scatter_about(seeds[0], (MEMBERS, LEVELS, GRID), 1.0, 6.0, ((0, 4), (2, 8)))
    eigvecs = scatter_about(seeds[1], (MODES, LEVELS, GRID), 1.0, 6.0, ((0, 4), (2, 8)))
    control = scatter_about(seeds[2], (MODES, MEMBERS), 1.0, 6.0, (), jnp.float32)
    columns = plant(jax.random.randint(seeds[3], (TILES * BLOCKS, PATCH), 0, TILE_COLS), jax.random.fold_in(seeds[3], 1), 0, TILE_COLS - 1).astype(jnp.int32)
    interpolation = scatter_about(seeds[4], (TILES * BLOCKS, LEVELS * PATCH, OBS_BLOCK), (LEVELS * PATCH) ** -0.5, 0.375, ((0, 8),))
    owners = draw_owners(jax.random.fold_in(seeds[8], 71), 0)
    innovation = scatter_about(seeds[6], (TILES, SLOTS, OBS_BLOCK), 1.0, 6.0, ((0, 8),), jnp.float32)
    obs_weight = jnp.clip(jnp.exp(math.log(4.0) - 2.7725887 * jax.random.uniform(seeds[7], (TILES, SLOTS, OBS_BLOCK), jnp.float32) ** levels(seeds[7], (TILES, SLOTS, OBS_BLOCK), ((0, 8),), -0.2, 0.2)), 0.25, 4.0)
    return dict(members=members, eigvecs=eigvecs, control=control, columns=columns, interpolation=interpolation, owners=owners, innovation=innovation, obs_weight=obs_weight)


def tile_image(args):
    field, cols, blocks = args
    picked = field[:, cols.reshape(-1)].reshape(LEVELS, BLOCKS, PATCH)
    picked = jnp.transpose(picked, (1, 0, 2)).reshape(BLOCKS, LEVELS * PATCH)
    return jnp.einsum('jr,jro->jo', picked.astype(jnp.float32), blocks.astype(jnp.float32))

def tile_adjoint(args):
    cols, blocks, back = args
    spread = jnp.einsum('jro,jo->jr', blocks.astype(jnp.float32), back.astype(jnp.float32))
    spread = jnp.transpose(spread.reshape(BLOCKS, LEVELS, PATCH), (1, 0, 2)).reshape(LEVELS, BLOCKS * PATCH)
    return jnp.zeros((LEVELS, TILE_COLS), jnp.float32).at[:, cols.reshape(-1)].add(spread)

def reference(members, eigvecs, control, columns, interpolation, owners, innovation, obs_weight):
    scale = 1.0 / math.sqrt(MODES * MEMBERS)
    control_b = control.astype(jnp.bfloat16)
    mixed = jnp.dot(control_b.T, eigvecs.reshape(MODES, -1), preferred_element_type=jnp.float32)
    increment = scale * lax.optimization_barrier(jnp.sum(members.reshape(MEMBERS, -1).astype(jnp.float32) * mixed, axis=0))
    increment_b = increment.astype(jnp.bfloat16).reshape(LEVELS, TILES, TILE_COLS)
    col_tiles = columns.reshape(TILES, BLOCKS, PATCH)
    block_tiles = interpolation.reshape(TILES, BLOCKS, LEVELS * PATCH, OBS_BLOCK)
    image = lax.map(tile_image, (jnp.transpose(increment_b, (1, 0, 2)), col_tiles, block_tiles))
    own = owners.reshape(TILES, BLOCKS)
    order = jnp.arange(BLOCKS, dtype=jnp.int32)
    earlier = order[None, :] < order[:, None]
    same = own[:, :, None] == own[:, None, :]
    rank = lax.optimization_barrier(jnp.sum(jnp.logical_and(same, earlier[None]), axis=2)).astype(jnp.int32)
    slot = (jnp.arange(TILES, dtype=jnp.int32)[:, None] * CAPACITY + rank).astype(jnp.int32)
    slot_image = jnp.zeros((TILES, SLOTS, OBS_BLOCK), jnp.float32).at[own, slot].set(image)
    live = jnp.zeros((TILES, SLOTS), jnp.float32).at[own, slot].set(1.0)
    departures = live[:, :, None] * obs_weight * (innovation - slot_image)
    departures_b = departures.astype(jnp.bfloat16)
    back = departures_b[own, slot]
    adjoint = lax.map(tile_adjoint, (col_tiles, block_tiles, back))
    adjoint = jnp.transpose(adjoint, (1, 0, 2)).reshape(-1)
    weighted = (members.reshape(MEMBERS, -1).astype(jnp.float32) * adjoint).astype(jnp.bfloat16)
    total = jnp.dot(eigvecs.reshape(MODES, -1), weighted.T, preferred_element_type=jnp.float32)
    gradient = control - scale * total
    return (gradient, departures)
```

```python
import functools
import math

import jax
import jax.numpy as jnp
from jax import lax
from jax.experimental import pallas as pl
from jax.experimental.pallas import tpu as pltpu
from jax.sharding import PartitionSpec as P

MESH = pl.DeviceIdType.MESH
CORES = 2
CHUNKS = 4
ADJ_CHUNKS = 2
LANES = 128
F32, BF16 = jnp.float32, jnp.bfloat16
HIGHEST = lax.Precision.HIGHEST


def greet(axes):
    barrier = pltpu.get_barrier_semaphore()
    total = 0
    for axis, size in axes:
        me = lax.axis_index(axis)
        for step in range(1, size):
            pl.semaphore_signal(
                barrier, inc=1, device_id={axis: lax.rem(me + step, size)}, device_id_type=MESH
            )
        total += size - 1
    pl.semaphore_wait(barrier, total)


def remote(src, dst, send, recv, axis, peer):
    copy = pltpu.make_async_remote_copy(
        src_ref=src, dst_ref=dst, send_sem=send, recv_sem=recv,
        device_id={axis: peer}, device_id_type=MESH,
    )
    copy.start()
    return copy


def iota(shape, dim):
    return lax.broadcasted_iota(jnp.int32, shape, dim)


def whole_kernel(
    nband, tiles, scale, mem_hbm, eig_hbm, control_hbm, cols_hbm, interp_hbm, owners_hbm,
    innov_hbm, obs_hbm, grad_ref, dep_ref,
    all_ref, eig_all, eig_wide, eig_lvl, control, cols, owners, mixed, mem_wide, mem_lvl,
    base, parts, select, interp, innov, obs, spread, image, send, upward, adj_out, adj_in,
    local, turned, sums,
    load_sem, mem_send, mem_recv, eig_send, eig_recv, far_send, far_recv,
    innov_send, innov_recv, obs_send, obs_recv, part_send, part_recv,
    dep_send, dep_recv, adj_send, adj_recv, turn_send, turn_recv, sum_send, sum_recv,
):
    me = lax.axis_index("band")
    tile = lax.axis_index("mem")
    chips = nband // CORES
    core = lax.rem(me, CORES)
    chip = lax.div(me, CORES)
    members, half, tile_cols = all_ref.shape
    mem_dev = members // nband
    modes_chip = eig_all.shape[0]
    modes_dev = modes_chip // CORES
    levels = half * CORES
    patch, blocks = cols.shape
    capacity, quarter = send.shape[1:]
    partner = me + 1 - 2 * core
    own_obs = pl.ds(pl.multiple_of(me * quarter, quarter), quarter)
    width = tile_cols // CHUNKS
    chunks = [slice(c * width, (c + 1) * width) for c in range(CHUNKS)]

    def halves(which):
        return pl.ds(pl.multiple_of(which * half, half), half)

    own_mem = all_ref.at[pl.ds(me * mem_dev, mem_dev)]
    own_eig = eig_all.at[pl.ds(core * modes_dev, modes_dev)]

    loads = [
        pltpu.make_async_copy(src, dst, load_sem.at[i])
        for i, (src, dst) in enumerate((
            (eig_hbm.at[:, halves(core)], own_eig),
            (control_hbm, control),
            (cols_hbm, cols),
            (owners_hbm, owners),
            (mem_hbm.at[:, halves(core)], own_mem),
            (interp_hbm.at[:, :, own_obs], interp),
            (innov_hbm.at[0, pl.ds(tile * capacity, capacity), own_obs], innov.at[tile]),
            (obs_hbm.at[0, pl.ds(tile * capacity, capacity), own_obs], obs.at[tile]),
        ))
    ]
    for copy in loads[:5]:
        copy.start()
    greet((("band", nband), ("mem", tiles)))
    far_copies = []
    for c, span in enumerate(chunks):
        step_copies = []
        for far in range(1, chips):
            for step in range(CORES):
                target = lax.rem(core + step, CORES)
                peer = lax.rem(chip + far, chips) * CORES + target
                step_copies.append(remote(
                    mem_hbm.at[:, halves(target), span],
                    all_ref.at[pl.ds(me * mem_dev, mem_dev), :, span],
                    far_send.at[c, far - 1, step], far_recv.at[c, far - 1, step], "band", peer,
                ))
        far_copies.append(step_copies)
    eig_copy = remote(
        eig_hbm.at[:, halves(1 - core)], own_eig, eig_send, eig_recv, "band", partner
    )
    mem_copy = remote(
        mem_hbm.at[:, halves(1 - core)], own_mem, mem_send, mem_recv, "band", partner
    )
    early = []
    for step in range(1, tiles):
        peer = lax.rem(tile + step, tiles)
        rows = pl.ds(pl.multiple_of(peer * capacity, capacity), capacity)
        early.append(remote(
            innov_hbm.at[0, rows, own_obs], innov.at[tile], innov_send.at[step - 1],
            innov_recv.at[step - 1], "mem", peer,
        ))
        early.append(remote(
            obs_hbm.at[0, rows, own_obs], obs.at[tile], obs_send.at[step - 1],
            obs_recv.at[step - 1], "mem", peer,
        ))
    for copy in loads[5:]:
        copy.start()
    for copy in loads[:5]:
        copy.wait()

    shape = (members * half, members)
    repeat = jnp.where(lax.div(iota(shape, 0), half) == iota(shape, 1), 1.0, 0.0).astype(BF16)
    rows_of = jnp.dot(repeat, control[...].astype(BF16), preferred_element_type=F32).astype(BF16)
    shape = (control.shape[1], modes_chip * half)
    widen = jnp.where(
        iota(shape, 0) == lax.div(iota(shape, 1), half) + chip * modes_chip, 1.0, 0.0
    ).astype(BF16)
    shape = (members * half, modes_chip * half)
    weight = jnp.where(
        lax.rem(iota(shape, 0), half) == lax.rem(iota(shape, 1), half),
        jnp.dot(rows_of, widen, preferred_element_type=F32), 0.0,
    ).astype(BF16)
    eig_copy.wait()
    for span in chunks:
        wide = eig_all[:, :, span].astype(F32)
        eig_wide[:, :, span] = wide
        mixed[:, :, span] = jnp.dot(
            weight, wide.reshape(modes_chip * half, width).astype(BF16),
            preferred_element_type=F32,
        ).reshape(members, half, width)
    mem_copy.wait()

    def chip_sum(which, span):
        rows = pl.ds(which * (mem_dev * CORES), mem_dev * CORES)
        wide = all_ref[rows, :, span].astype(F32)
        mem_wide[rows, :, span] = wide
        return jnp.sum(wide * mixed[rows, :, span], axis=0)

    for span in chunks:
        base[:, span] = chip_sum(chip, span)
    for level in range(half):
        eig_lvl[level] = eig_wide[:, level, :].astype(BF16)

    per_row = LANES // levels
    groups = blocks // per_row
    column = iota((patch, tile_cols), 1)

    def row_of(j):
        return (lax.rem(j, per_row) * groups + lax.div(j, per_row)) * patch

    for j in range(blocks):
        row = ((j % per_row) * groups + j // per_row) * patch
        select[row : row + patch] = jnp.where(
            cols[:, j : j + 1] == column, 1.0, 0.0
        ).astype(BF16)
    per_lane = owners.shape[1] // blocks
    line = owners[pl.ds(lax.div(tile, per_lane), 1)]
    owner = line[:, :blocks]
    for i in range(1, per_lane):
        owner = jnp.where(
            lax.rem(tile, per_lane) == i, line[:, i * blocks : (i + 1) * blocks], owner
        )
    owner = owner.astype(F32)
    down, across = iota((blocks, blocks), 0), iota((blocks, blocks), 1)
    owner_column = jnp.sum(jnp.where(down == across, owner, 0.0), axis=1, keepdims=True)
    same = jnp.where(jnp.logical_and(owner_column == owner, down < across), 1.0, 0.0)
    rank = jnp.sum(same, axis=0, keepdims=True)
    target = (owner * capacity + rank).astype(jnp.int32)
    placing = jnp.where(iota((tiles * capacity, blocks), 0) == target, 1.0, 0.0)
    for copy in loads[5:]:
        copy.wait()
    for copy in early:
        copy.wait()

    def at_blocks(ref):
        return lax.dot_general(
            placing, ref[...].reshape(tiles * capacity, quarter), (((0,), (0,)), ((), ())),
            precision=HIGHEST, preferred_element_type=F32,
        )

    innov_block = at_blocks(innov)
    obs_block = at_blocks(obs)

    def gather(c):
        span = chunks[c]
        for copy in part_copies[c]:
            copy.wait()
        sides = []
        for side in range(CORES):
            total = parts[side, :, span]
            for other in range(1, chips):
                total = total + parts[other * CORES + side, :, span]
            sides.append((scale * total).astype(BF16).astype(F32))
        increment = jnp.concatenate(sides, axis=0).astype(BF16)
        value = lax.dot_general(
            select[:, span], increment, (((1,), (1,)), ((), ())), preferred_element_type=F32
        )
        if c == 0:
            spread[...] = value
        else:
            spread[...] += value

    part_copies = []
    for c, span in enumerate(chunks):
        for copy in far_copies[c]:
            copy.wait()
        total = base[:, span]
        for far in range(1, chips):
            total = total + chip_sum(lax.rem(chip + far, chips), span)
        parts[me, :, span] = total
        copies = []
        for step in range(1, nband):
            block = parts.at[me, :, span]
            copies.append(remote(
                block, block, part_send.at[c, step - 1], part_recv.at[c, step - 1],
                "band", lax.rem(me + step, nband),
            ))
        part_copies.append(copies)
        if c:
            gather(c - 1)
        for level in range(half):
            mem_lvl[level, :, span] = mem_wide[:, level, span]
    gather(CHUNKS - 1)

    def project(j, carry):
        value = spread[pl.ds(pl.multiple_of(row_of(j), patch), patch)]
        total = jnp.zeros((patch, quarter), F32)
        for level in range(levels):
            total += value[:, level : level + 1] * interp[
                j, level * patch : (level + 1) * patch
            ].astype(F32)
        image[pl.ds(j, 1)] = jnp.sum(total, axis=0, keepdims=True)
        return carry

    lax.fori_loop(0, blocks, project, 0, unroll=4)
    departure = obs_block * (innov_block - image[...])
    image[...] = departure

    lane = iota((patch, LANES), 1)
    turn = lax.rem(lax.div(iota((LANES, quarter), 0), levels), 2)

    def gather_up(g, carry):
        total = jnp.zeros((patch, LANES), F32)
        for pair in range(per_row // 2):
            sides, facing = [], []
            for k in range(2):
                j = g * per_row + 2 * pair + k
                sides.append(interp[j])
                own = jnp.broadcast_to(image[pl.ds(j, 1)], (LANES, quarter))
                facing.append(jnp.where(turn == k, own, 0.0).astype(BF16))
            value = lax.dot_general(
                jnp.concatenate(sides, axis=1), jnp.concatenate(facing, axis=1),
                (((1,), (1,)), ((), ())), preferred_element_type=F32,
            )
            for level in range(levels):
                here = jnp.logical_and(
                    lax.div(lane, 2 * levels) == pair, lax.rem(lane, levels) == level
                )
                total = jnp.where(here, value[level * patch : (level + 1) * patch], total)
        upward[pl.ds(pl.multiple_of(g * patch, patch), patch)] = total
        return carry

    lax.fori_loop(0, groups, gather_up, 0)
    turned_up = upward[...].T
    high = turned_up.astype(BF16)
    low = (turned_up - high.astype(F32)).astype(BF16)
    left = jnp.concatenate([
        jnp.concatenate([x[i * levels : (i + 1) * levels] for i in range(per_row)], axis=1)
        for x in (high, low)
    ], axis=0)
    adj_width = tile_cols // ADJ_CHUNKS
    adj_spans = [slice(c * adj_width, (c + 1) * adj_width) for c in range(ADJ_CHUNKS)]
    adj_copies = []
    for c, span in enumerate(adj_spans):
        value = jnp.dot(left, select[:, span], preferred_element_type=F32)
        value = value[:levels] + value[levels:]
        for side in range(CORES):
            adj_out[side, :, span] = value[side * half : (side + 1) * half]
        copies = []
        for step in range(1, nband):
            peer = lax.rem(me + step, nband)
            copies.append(remote(
                adj_out.at[lax.rem(peer, CORES), :, span], adj_in.at[me, :, span],
                adj_send.at[c, step - 1], adj_recv.at[c, step - 1], "band", peer,
            ))
        adj_copies.append(copies)

    send[...] = jnp.dot(
        placing, image[...], precision=HIGHEST, preferred_element_type=F32
    ).reshape(send.shape)
    own_slots = pl.ds(pl.multiple_of(tile * capacity, capacity), capacity)
    dep_copies = []
    for step in range(1, tiles):
        peer = lax.rem(tile + step, tiles)
        dep_copies.append(remote(
            send.at[peer], dep_ref.at[0, own_slots], dep_send.at[step - 1],
            dep_recv.at[step - 1], "mem", peer,
        ))
    dep_ref[0, own_slots] = send[tile]
    local[...] = jnp.zeros_like(local)

    total = None
    for c, span in enumerate(adj_spans):
        for copy in adj_copies[c]:
            copy.wait()
        adjoint = adj_out[core, :, span]
        for step in range(1, nband):
            adjoint = adjoint + adj_in[lax.rem(me + step, nband), :, span]
        for level in range(half):
            weighted = (mem_lvl[level, :, span] * adjoint[level : level + 1]).astype(BF16)
            term = lax.dot_general(
                weighted, eig_lvl[level, :, span], (((1,), (1,)), ((), ())),
                preferred_element_type=F32,
            )
            total = term if total is None else total + term
    for b in range(nband):
        local[b, :, :modes_chip] = total[b * mem_dev : (b + 1) * mem_dev]
    copies = []
    for step in range(1, nband):
        peer = lax.rem(me + step, nband)
        copies.append(remote(
            local.at[peer], turned.at[me], turn_send.at[step - 1], turn_recv.at[step - 1],
            "band", peer,
        ))
    turned[me] = local[me]
    for copy in copies:
        copy.wait()
    own = None
    for b in range(nband):
        value = turned[b]
        if b >= CORES:
            value = pltpu.roll(value, (b // CORES) * modes_chip, 1)
        own = value if own is None else own + value
    sums[tile] = own
    copies = []
    for step in range(1, tiles):
        peer = lax.rem(tile + step, tiles)
        copies.append(remote(
            sums.at[tile], sums.at[tile], sum_send.at[step - 1], sum_recv.at[step - 1],
            "mem", peer,
        ))
    for copy in copies:
        copy.wait()
    whole = sums[0]
    for t in range(1, tiles):
        whole = whole + sums[t]
    grad_ref[...] = (
        control[pl.ds(pl.multiple_of(me * mem_dev, mem_dev), mem_dev)]
        - scale * whole[:, : grad_ref.shape[1]]
    )
    for copy in dep_copies:
        copy.wait()


def dma(*shape):
    return pltpu.SemaphoreType.DMA(shape)


def per_device(members, eigvecs, control, columns, interpolation, owners, innovation, obs_weight):
    nband = lax.axis_size("band")
    tiles = lax.axis_size("mem")
    mem_dev, levels, tile_cols = members.shape
    own_modes = eigvecs.shape[0]
    blocks, patch = columns.shape
    obs_block = interpolation.shape[2]
    capacity = innovation.shape[1] // tiles
    modes, total_members = control.shape
    scale = 1.0 / math.sqrt(modes * total_members)
    quarter = obs_block // nband
    half = levels // CORES
    chips = nband // CORES
    modes_chip = own_modes * CORES
    group_rows = blocks * levels // LANES * patch
    lanes = pl.cdiv(modes, LANES) * LANES
    slots = (tiles, capacity, quarter)
    own_slots = (1, tiles * capacity, quarter)
    owner_rows = owners.reshape(owners.shape[0] // LANES, LANES)
    hbm = pl.BlockSpec(memory_space=pltpu.HBM)
    vmem = pl.BlockSpec(memory_space=pltpu.VMEM)
    operands = (
        members, eigvecs, control.T, columns.T, interpolation, owner_rows, innovation, obs_weight
    )
    gradient, departure = pl.pallas_call(
        functools.partial(whole_kernel, nband, tiles, scale),
        out_shape=(
            jax.ShapeDtypeStruct((mem_dev, modes), F32),
            jax.ShapeDtypeStruct(own_slots, F32),
        ),
        in_specs=[hbm] * len(operands),
        out_specs=(vmem, vmem),
        scratch_shapes=[
            pltpu.VMEM((total_members, half, tile_cols), BF16),
            pltpu.VMEM((modes_chip, half, tile_cols), BF16),
            pltpu.VMEM((modes_chip, half, tile_cols), F32),
            pltpu.VMEM((half, modes_chip, tile_cols), BF16),
            pltpu.VMEM((total_members, modes), F32),
            pltpu.VMEM((patch, blocks), jnp.int32),
            pltpu.VMEM(owner_rows.shape, jnp.int32),
            pltpu.VMEM((total_members, half, tile_cols), F32),
            pltpu.VMEM((total_members, half, tile_cols), F32),
            pltpu.VMEM((half, total_members, tile_cols), F32),
            pltpu.VMEM((half, tile_cols), F32),
            pltpu.VMEM((nband, half, tile_cols), F32),
            pltpu.VMEM((blocks * patch, tile_cols), BF16),
            pltpu.VMEM((blocks, levels * patch, quarter), BF16),
            pltpu.VMEM(slots, F32),
            pltpu.VMEM(slots, F32),
            pltpu.VMEM((blocks * patch, levels), F32),
            pltpu.VMEM((blocks, quarter), F32),
            pltpu.VMEM(slots, F32),
            pltpu.VMEM((group_rows, LANES), F32),
            pltpu.VMEM((CORES, half, tile_cols), F32),
            pltpu.VMEM((nband, half, tile_cols), F32),
            pltpu.VMEM((nband, mem_dev, lanes), F32),
            pltpu.VMEM((nband, mem_dev, lanes), F32),
            pltpu.VMEM((tiles, mem_dev, lanes), F32),
            dma(8), dma(), dma(), dma(), dma(),
            dma(CHUNKS, chips - 1, CORES), dma(CHUNKS, chips - 1, CORES),
            dma(tiles - 1), dma(tiles - 1), dma(tiles - 1), dma(tiles - 1),
            dma(CHUNKS, nband - 1), dma(CHUNKS, nband - 1),
            dma(tiles - 1), dma(tiles - 1),
            dma(ADJ_CHUNKS, nband - 1), dma(ADJ_CHUNKS, nband - 1),
            dma(nband - 1), dma(nband - 1), dma(tiles - 1), dma(tiles - 1),
        ],
        compiler_params=pltpu.CompilerParams(
            collective_id=1, has_side_effects=True, vmem_limit_bytes=40 << 20
        ),
    )(*[pltpu.with_memory_space_constraint(x, pltpu.HBM) for x in operands])
    return (gradient.T, departure)


def solution(mesh):
    return jax.shard_map(
        per_device,
        mesh=mesh,
        in_specs=(
            P("band", None, "mem"),
            P("band", None, "mem"),
            P(),
            P("mem", None),
            P("mem", None, None),
            P(),
            P("mem", None, None),
            P("mem", None, None),
        ),
        out_specs=(P(None, "band"), P("mem", None, "band")),
        check_vma=False,
    )
```

```python
import functools
import math

import jax
import jax.numpy as jnp
from jax import lax
from jax.experimental import pallas as pl
from jax.experimental.pallas import tpu as pltpu
from jax.sharding import PartitionSpec as P

MESH = pl.DeviceIdType.MESH
CORES = 2
SUB = 8
DEPTH = 256
SPANS = 2
AHEAD = 2
LANES = 128
F32, BF16 = jnp.float32, jnp.bfloat16
HIGHEST = lax.Precision.HIGHEST


def flip(index, bit):
    return index + bit * (1 - 2 * lax.rem(lax.div(index, bit), 2))


def signal(semaphore, axis, peer):
    pl.semaphore_signal(semaphore, inc=1, device_id={axis: peer}, device_id_type=MESH)


def remote(src, dst, send, recv, axis, peer):
    copy = pltpu.make_async_remote_copy(
        src_ref=src, dst_ref=dst, send_sem=send, recv_sem=recv,
        device_id={axis: peer}, device_id_type=MESH,
    )
    copy.start()
    return copy


def iota(shape, dim):
    return lax.broadcasted_iota(jnp.int32, shape, dim)


def whole_kernel(
    nband, tiles, scale, mem_hbm, eig_hbm, control_hbm, cols_hbm, interp_hbm, owners_hbm,
    innov_hbm, obs_hbm, grad_ref, dep_ref,
    all_ref, eig_all, eig_wide, eig_lvl, control, cols, owners, mixed, mem_wide, mem_lvl,
    base, parts, select, interp, innov, obs, spread, image, send, upward, adj_out, adj_in,
    local, turned, sums, meet,
    load_sem, mem_send, mem_recv, eig_send, eig_recv, far_send, far_recv,
    innov_send, innov_recv, obs_send, obs_recv, part_send, part_recv,
    dep_send, dep_recv, adj_send, adj_recv, turn_send, turn_recv, sum_send, sum_recv,
):
    me = lax.axis_index("band")
    tile = lax.axis_index("mem")
    chips = nband // CORES
    core = lax.rem(me, CORES)
    chip = lax.div(me, CORES)
    subs, members, _, half = all_ref.shape
    mem_dev = members // nband
    mem_chip = mem_dev * CORES
    modes_chip = eig_all.shape[1]
    modes_dev = modes_chip // CORES
    levels = subs * SUB
    patch, blocks = cols.shape
    capacity, quarter = send.shape[1:]
    rounds = meet.shape[0]
    partner = me + 1 - 2 * core
    own_obs = pl.ds(pl.multiple_of(me * quarter, quarter), quarter)
    width = half // SPANS
    spans = [slice(c * width, (c + 1) * width) for c in range(SPANS)]
    chunks = [(sub, span) for sub in range(subs) for span in spans]

    def rows_of_sub(sub):
        return slice(sub * SUB, (sub + 1) * SUB)

    def columns_of(which, span=slice(0, None)):
        start = span.start
        size = (half if span.stop is None else span.stop) - start
        return pl.ds(pl.multiple_of(which * half + start, size), size)

    own_mem = pl.ds(me * mem_dev, mem_dev)
    own_eig = pl.ds(core * modes_dev, modes_dev)

    pairs = [
        (eig_hbm.at[:, rows_of_sub(sub), columns_of(core)], eig_all.at[sub, own_eig])
        for sub in range(subs)
    ] + [(control_hbm, control), (cols_hbm, cols), (owners_hbm, owners)] + [
        (mem_hbm.at[:, rows_of_sub(sub), columns_of(core)], all_ref.at[sub, own_mem])
        for sub in range(subs)
    ] + [
        (interp_hbm.at[:, :, own_obs], interp),
        (innov_hbm.at[0, pl.ds(tile * capacity, capacity), own_obs], innov.at[tile]),
        (obs_hbm.at[0, pl.ds(tile * capacity, capacity), own_obs], obs.at[tile]),
    ]
    loads = [
        pltpu.make_async_copy(src, dst, load_sem.at[i]) for i, (src, dst) in enumerate(pairs)
    ]
    late = len(loads) - 3
    for copy in loads[:late]:
        copy.start()

    barrier = pltpu.get_barrier_semaphore()
    for step in range(1, nband):
        signal(barrier, "band", lax.rem(me + step, nband))
    for i in range(rounds):
        signal(barrier, "mem", flip(tile, 1 << i))
    pl.semaphore_wait(barrier, nband - 1 + rounds)

    far_copies = []

    def send_members(c):
        sub, span = chunks[c]
        copies = []
        for far in range(1, chips):
            for step in range(CORES):
                target = lax.rem(core + step, CORES)
                peer = lax.rem(chip + far, chips) * CORES + target
                copies.append(remote(
                    mem_hbm.at[:, rows_of_sub(sub), columns_of(target, span)],
                    all_ref.at[sub, own_mem, :, span],
                    far_send.at[c, far - 1, step], far_recv.at[c, far - 1, step], "band", peer,
                ))
        far_copies.append(copies)

    for c in range(AHEAD):
        send_members(c)
    eig_copies = [
        remote(
            eig_hbm.at[:, rows_of_sub(sub), columns_of(1 - core)], eig_all.at[sub, own_eig],
            eig_send.at[sub], eig_recv.at[sub], "band", partner,
        )
        for sub in range(subs)
    ]
    mem_copies = [
        remote(
            mem_hbm.at[:, rows_of_sub(sub), columns_of(1 - core)], all_ref.at[sub, own_mem],
            mem_send.at[sub], mem_recv.at[sub], "band", partner,
        )
        for sub in range(subs)
    ]
    for copy in loads[late:]:
        copy.start()
    for i in range(rounds):
        signal(meet.at[i], "mem", flip(tile, 1 << i))
        pl.semaphore_wait(meet.at[i], 1)
    early = []
    for step in range(1, tiles):
        peer = lax.rem(tile + step, tiles)
        rows = pl.ds(pl.multiple_of(peer * capacity, capacity), capacity)
        early.append(remote(
            innov_hbm.at[0, rows, own_obs], innov.at[tile], innov_send.at[step - 1],
            innov_recv.at[step - 1], "mem", peer,
        ))
        early.append(remote(
            obs_hbm.at[0, rows, own_obs], obs.at[tile], obs_send.at[step - 1],
            obs_recv.at[step - 1], "mem", peer,
        ))
    for copy in loads[:late]:
        copy.wait()

    shape = (members * SUB, members)
    repeat = jnp.where(lax.div(iota(shape, 0), SUB) == iota(shape, 1), 1.0, 0.0).astype(BF16)
    rows_of = jnp.dot(repeat, control[...].astype(BF16), preferred_element_type=F32).astype(BF16)
    shape = (control.shape[1], modes_chip * SUB)
    widen = jnp.where(
        iota(shape, 0) == lax.div(iota(shape, 1), SUB) + chip * modes_chip, 1.0, 0.0
    ).astype(BF16)
    shape = (members * SUB, modes_chip * SUB)
    weight = jnp.where(
        lax.rem(iota(shape, 0), SUB) == lax.rem(iota(shape, 1), SUB),
        jnp.dot(rows_of, widen, preferred_element_type=F32), 0.0,
    ).astype(BF16)

    def chip_sum(which, sub, span):
        rows = pl.ds(which * mem_chip, mem_chip)
        wide = all_ref[sub, rows, :, span].astype(F32)
        mem_wide[sub, rows, :, span] = wide
        return jnp.sum(wide * mixed[sub, rows, :, span], axis=0)

    for sub in range(subs):
        eig_copies[sub].wait()
        mem_copies[sub].wait()
        for span in spans:
            wide = eig_all[sub, :, :, span].astype(F32)
            eig_wide[sub, :, :, span] = wide
            mixed[sub, :, :, span] = jnp.dot(
                weight, wide.reshape(modes_chip * SUB, width).astype(BF16),
                preferred_element_type=F32,
            ).reshape(members, SUB, width)
            base[sub, :, span] = chip_sum(chip, sub, span)

    column = iota((patch, half * CORES), 1)
    for j in range(blocks):
        select[j * patch : (j + 1) * patch] = jnp.where(
            cols[:, j : j + 1] == column, 1.0, 0.0
        ).astype(BF16)

    part_copies = []

    def finish(c):
        sub, span = chunks[c]
        for copy in far_copies[c]:
            copy.wait()
        total = base[sub, :, span]
        for far in range(1, chips):
            total = total + chip_sum(lax.rem(chip + far, chips), sub, span)
        parts[me, sub, :, span] = total
        copies = []
        for step in range(1, nband):
            block = parts.at[me, sub, :, span]
            copies.append(remote(
                block, block, part_send.at[c, step - 1], part_recv.at[c, step - 1],
                "band", lax.rem(me + step, nband),
            ))
        part_copies.append(copies)
        if c + AHEAD < len(chunks):
            send_members(c + AHEAD)

    def gather(c):
        sub, span = chunks[c]
        for copy in part_copies[c]:
            copy.wait()
        value = None
        for side in range(CORES):
            total = parts[side, sub, :, span]
            for other in range(1, chips):
                total = total + parts[other * CORES + side, sub, :, span]
            term = lax.dot_general(
                (scale * total).astype(BF16),
                select[:, side * half + span.start : side * half + span.stop],
                (((1,), (1,)), ((), ())), preferred_element_type=F32,
            )
            value = term if value is None else value + term
        if span.start == 0:
            spread[rows_of_sub(sub)] = value
        else:
            spread[rows_of_sub(sub)] += value

    per_group = DEPTH // patch
    groups = blocks // per_group
    diagonal = lax.div(iota((per_group, DEPTH), 1), patch) == iota((per_group, DEPTH), 0)

    def blocks_of(group, level):
        return jnp.concatenate([
            interp[
                group * per_group : (group + 1) * per_group, at * patch : (at + 1) * patch
            ].reshape(DEPTH, quarter)
            for at in (level, level + 1)
        ], axis=1)

    def project(sub):
        for group in range(groups):
            lanes = slice(group * DEPTH, (group + 1) * DEPTH)
            total = None
            for level in range(sub * SUB, (sub + 1) * SUB, 2):
                left = jnp.concatenate([
                    jnp.where(diagonal, spread[at : at + 1, lanes], 0.0)
                    for at in (level, level + 1)
                ], axis=0).astype(BF16)
                term = jnp.dot(left, blocks_of(group, level), preferred_element_type=F32)
                total = term if total is None else total + term
            value = total[:per_group, :quarter] + total[per_group:, quarter:]
            rows = slice(group * per_group, (group + 1) * per_group)
            if sub == 0:
                image[rows] = value
            else:
                image[rows] += value

    def spread_members(c):
        sub, span = chunks[c]
        for level in range(SUB):
            mem_lvl[sub * SUB + level, :, span] = mem_wide[sub, :, level, span]

    finish(0)
    for sub in range(subs):
        for level in range(SUB):
            eig_lvl[sub * SUB + level] = eig_wide[sub, :, level, :].astype(BF16)
    spread_members(0)

    finish(1)
    per_lane = owners.shape[1] // blocks
    line = owners[pl.ds(lax.div(tile, per_lane), 1)]
    owner = line[:, :blocks]
    for i in range(1, per_lane):
        owner = jnp.where(
            lax.rem(tile, per_lane) == i, line[:, i * blocks : (i + 1) * blocks], owner
        )
    owner = owner.astype(F32)
    down, across = iota((blocks, blocks), 0), iota((blocks, blocks), 1)
    owner_column = jnp.sum(jnp.where(down == across, owner, 0.0), axis=1, keepdims=True)
    same = jnp.where(jnp.logical_and(owner_column == owner, down < across), 1.0, 0.0)
    rank = jnp.sum(same, axis=0, keepdims=True)
    target = (owner * capacity + rank).astype(jnp.int32)
    placing = jnp.where(iota((tiles * capacity, blocks), 0) == target, 1.0, 0.0)
    for copy in loads[late:]:
        copy.wait()
    for copy in early:
        copy.wait()

    def at_blocks(ref):
        return lax.dot_general(
            placing, ref[...].reshape(tiles * capacity, quarter), (((0,), (0,)), ((), ())),
            precision=HIGHEST, preferred_element_type=F32,
        )

    innov_block = at_blocks(innov)
    obs_block = at_blocks(obs)
    gather(0)
    spread_members(1)

    done = 0
    for c in range(2, len(chunks)):
        finish(c)
        gather(c - 1)
        if chunks[c - 1][0] != chunks[c][0]:
            project(chunks[c - 1][0])
            done = chunks[c][0]
        spread_members(c)
    gather(len(chunks) - 1)
    project(done)
    departure = obs_block * (innov_block - image[...])
    image[...] = departure

    rounded = departure.astype(BF16)
    blank = jnp.zeros((per_group, quarter), BF16)
    for group in range(groups):
        own = rounded[group * per_group : (group + 1) * per_group]
        left = jnp.concatenate([
            jnp.concatenate([own, blank], axis=1), jnp.concatenate([blank, own], axis=1)
        ], axis=0)
        for level in range(0, levels, 2):
            value = lax.dot_general(
                left, blocks_of(group, level), (((1,), (1,)), ((), ())),
                preferred_element_type=F32,
            )
            for k in range(2):
                upward[level + k : level + k + 1, group * DEPTH : (group + 1) * DEPTH] = jnp.sum(
                    jnp.where(diagonal, value[k * per_group : (k + 1) * per_group], 0.0),
                    axis=0, keepdims=True,
                )
    high = upward[...].astype(BF16)
    low = (upward[...] - high.astype(F32)).astype(BF16)
    left = jnp.concatenate([high, low], axis=0)
    far_peers = [lax.rem(chip + far, chips) * CORES for far in range(1, chips)]
    adj_copies = []
    for c, span in enumerate(spans):
        copies = []
        for own in range(CORES):
            side = core if own else 1 - core
            value = jnp.dot(
                left, select[:, columns_of(side, span)], preferred_element_type=F32
            )
            adj_out[own, :, span] = value[:levels] + value[levels:]
            peers = [peer + side for peer in far_peers]
            if not own:
                peers = [partner] + peers
            for peer in peers:
                k = len(copies)
                copies.append(remote(
                    adj_out.at[own, :, span], adj_in.at[k, :, span],
                    adj_send.at[c, k], adj_recv.at[c, k], "band", peer,
                ))
        adj_copies.append(copies)

    send[...] = jnp.dot(
        placing, image[...], precision=HIGHEST, preferred_element_type=F32
    ).reshape(send.shape)
    own_slots = pl.ds(pl.multiple_of(tile * capacity, capacity), capacity)
    dep_copies = []
    for step in range(1, tiles):
        peer = lax.rem(tile + step, tiles)
        dep_copies.append(remote(
            send.at[peer], dep_ref.at[0, own_slots], dep_send.at[step - 1],
            dep_recv.at[step - 1], "mem", peer,
        ))
    dep_ref[0, own_slots] = send[tile]
    local[...] = jnp.zeros_like(local)

    total = None
    for c, span in enumerate(spans):
        for copy in adj_copies[c]:
            copy.wait()
        adjoint = adj_out[1, :, span]
        for k in range(nband - 1):
            adjoint = adjoint + adj_in[k, :, span]
        for level in range(levels):
            weighted = (mem_lvl[level, :, span] * adjoint[level : level + 1]).astype(BF16)
            term = lax.dot_general(
                weighted, eig_lvl[level, :, span], (((1,), (1,)), ((), ())),
                preferred_element_type=F32,
            )
            total = term if total is None else total + term
    for b in range(nband):
        local[b, :, :modes_chip] = total[b * mem_dev : (b + 1) * mem_dev]
    copies = []
    for step in range(1, nband):
        peer = lax.rem(me + step, nband)
        copies.append(remote(
            local.at[peer], turned.at[me], turn_send.at[step - 1], turn_recv.at[step - 1],
            "band", peer,
        ))
    turned[me] = local[me]
    for copy in copies:
        copy.wait()
    own = None
    for b in range(nband):
        value = turned[b]
        if b >= CORES:
            value = pltpu.roll(value, (b // CORES) * modes_chip, 1)
        own = value if own is None else own + value
    sums[tile] = own
    copies = []
    for step in range(1, tiles):
        peer = lax.rem(tile + step, tiles)
        copies.append(remote(
            sums.at[tile], sums.at[tile], sum_send.at[step - 1], sum_recv.at[step - 1],
            "mem", peer,
        ))
    for copy in copies:
        copy.wait()
    whole = sums[0]
    for t in range(1, tiles):
        whole = whole + sums[t]
    grad_ref[...] = (
        control[pl.ds(pl.multiple_of(me * mem_dev, mem_dev), mem_dev)]
        - scale * whole[:, : grad_ref.shape[1]]
    )
    for copy in dep_copies:
        copy.wait()


def dma(*shape):
    return pltpu.SemaphoreType.DMA(shape)


def per_device(members, eigvecs, control, columns, interpolation, owners, innovation, obs_weight):
    nband = lax.axis_size("band")
    tiles = lax.axis_size("mem")
    mem_dev, levels, tile_cols = members.shape
    own_modes = eigvecs.shape[0]
    blocks, patch = columns.shape
    obs_block = interpolation.shape[2]
    capacity = innovation.shape[1] // tiles
    modes, total_members = control.shape
    scale = 1.0 / math.sqrt(modes * total_members)
    quarter = obs_block // nband
    half = tile_cols // CORES
    subs = levels // SUB
    chips = nband // CORES
    modes_chip = own_modes * CORES
    rounds = (tiles - 1).bit_length()
    lanes = pl.cdiv(modes, LANES) * LANES
    slots = (tiles, capacity, quarter)
    own_slots = (1, tiles * capacity, quarter)
    owner_rows = owners.reshape(owners.shape[0] // LANES, LANES)
    hbm = pl.BlockSpec(memory_space=pltpu.HBM)
    vmem = pl.BlockSpec(memory_space=pltpu.VMEM)
    operands = (
        members, eigvecs, control.T, columns.T, interpolation, owner_rows, innovation, obs_weight
    )
    gradient, departure = pl.pallas_call(
        functools.partial(whole_kernel, nband, tiles, scale),
        out_shape=(
            jax.ShapeDtypeStruct((mem_dev, modes), F32),
            jax.ShapeDtypeStruct(own_slots, F32),
        ),
        in_specs=[hbm] * len(operands),
        out_specs=(vmem, vmem),
        scratch_shapes=[
            pltpu.VMEM((subs, total_members, SUB, half), BF16),
            pltpu.VMEM((subs, modes_chip, SUB, half), BF16),
            pltpu.VMEM((subs, modes_chip, SUB, half), F32),
            pltpu.VMEM((levels, modes_chip, half), BF16),
            pltpu.VMEM((total_members, modes), F32),
            pltpu.VMEM((patch, blocks), jnp.int32),
            pltpu.VMEM(owner_rows.shape, jnp.int32),
            pltpu.VMEM((subs, total_members, SUB, half), F32),
            pltpu.VMEM((subs, total_members, SUB, half), F32),
            pltpu.VMEM((levels, total_members, half), F32),
            pltpu.VMEM((subs, SUB, half), F32),
            pltpu.VMEM((nband, subs, SUB, half), F32),
            pltpu.VMEM((blocks * patch, tile_cols), BF16),
            pltpu.VMEM((blocks, levels * patch, quarter), BF16),
            pltpu.VMEM(slots, F32),
            pltpu.VMEM(slots, F32),
            pltpu.VMEM((levels, blocks * patch), F32),
            pltpu.VMEM((blocks, quarter), F32),
            pltpu.VMEM(slots, F32),
            pltpu.VMEM((levels, blocks * patch), F32),
            pltpu.VMEM((CORES, levels, half), F32),
            pltpu.VMEM((nband - 1, levels, half), F32),
            pltpu.VMEM((nband, mem_dev, lanes), F32),
            pltpu.VMEM((nband, mem_dev, lanes), F32),
            pltpu.VMEM((tiles, mem_dev, lanes), F32),
            pltpu.SemaphoreType.REGULAR((rounds,)),
            dma(6 + 2 * subs), dma(subs), dma(subs), dma(subs), dma(subs),
            dma(subs * SPANS, chips - 1, CORES), dma(subs * SPANS, chips - 1, CORES),
            dma(tiles - 1), dma(tiles - 1), dma(tiles - 1), dma(tiles - 1),
            dma(subs * SPANS, nband - 1), dma(subs * SPANS, nband - 1),
            dma(tiles - 1), dma(tiles - 1),
            dma(SPANS, nband - 1), dma(SPANS, nband - 1),
            dma(nband - 1), dma(nband - 1), dma(tiles - 1), dma(tiles - 1),
        ],
        compiler_params=pltpu.CompilerParams(
            collective_id=1, has_side_effects=True, vmem_limit_bytes=40 << 20
        ),
    )(*[pltpu.with_memory_space_constraint(x, pltpu.HBM) for x in operands])
    return (gradient.T, departure)


def solution(mesh):
    return jax.shard_map(
        per_device,
        mesh=mesh,
        in_specs=(
            P("band", None, "mem"),
            P("band", None, "mem"),
            P(),
            P("mem", None),
            P("mem", None, None),
            P(),
            P("mem", None, None),
            P("mem", None, None),
        ),
        out_specs=(P(None, "band"), P("mem", None, "band")),
        check_vma=False,
    )
```

```python
import functools
import math

import jax
import jax.numpy as jnp
from jax import lax
from jax.experimental import pallas as pl
from jax.experimental.pallas import tpu as pltpu
from jax.sharding import PartitionSpec as P

MESH = pl.DeviceIdType.MESH
CORES = 2
SUB = 8
DEPTH = 256
SPANS = 2
LANES = 128
F32, BF16 = jnp.float32, jnp.bfloat16
HIGHEST = lax.Precision.HIGHEST


def snake(index):
    row, column = lax.div(index, 2), lax.rem(index, 2)
    return index + lax.rem(row, 2) * (1 - 2 * column)


def signal(semaphore, axis, peer):
    pl.semaphore_signal(semaphore, inc=1, device_id={axis: peer}, device_id_type=MESH)


def signal_beside(semaphore, place, reach, size):
    def inform(there):
        @pl.when(jnp.logical_and(there >= 0, there < size))
        def _():
            signal(semaphore, "mem", snake(there))

    inform(place - reach)
    inform(place + reach)
    below = jnp.where(place >= reach, 1, 0)
    return below + jnp.where(place + reach < size, 1, 0)


def await_bytes(ref, semaphore):
    pltpu.make_async_copy(ref, ref, semaphore).wait()


def remote(src, dst, send, recv, **device):
    pltpu.make_async_remote_copy(
        src_ref=src, dst_ref=dst, send_sem=send, recv_sem=recv,
        device_id=device, device_id_type=MESH,
    ).start()


def iota(shape, dim):
    return lax.broadcasted_iota(jnp.int32, shape, dim)


def whole_kernel(
    nband, tiles, scale, mem_hbm, eig_hbm, control_hbm, cols_hbm, interp_hbm, owners_hbm,
    innov_hbm, obs_hbm, grad_ref, dep_ref,
    all_ref, eig_all, eig_wide, eig_lvl, control, cols, owners, mixed, mem_wide, mem_lvl,
    base, parts, select, interp, innov, obs, spread, image, send, upward, adj_out, adj_in,
    local, packed, terms, meet,
    load_sem, mem_recv, eig_recv, far_recv, part_recv, adj_recv,
    innov_recv, obs_recv, dep_recv, sum_recv,
    mem_send, eig_send, far_send, part_send, adj_send,
    innov_send, obs_send, dep_send, sum_send,
):
    me = lax.axis_index("band")
    tile = lax.axis_index("mem")
    chips = nband // CORES
    core = lax.rem(me, CORES)
    chip = lax.div(me, CORES)
    subs, members, _, half = all_ref.shape
    mem_dev = members // nband
    mem_chip = mem_dev * CORES
    modes_chip = eig_all.shape[1]
    modes_dev = modes_chip // CORES
    levels = subs * SUB
    patch, blocks = cols.shape
    capacity, quarter = send.shape[1:]
    rounds = meet.shape[0]
    partner = me + 1 - 2 * core
    own_obs = pl.ds(pl.multiple_of(me * quarter, quarter), quarter)
    width = half // SPANS
    spans = [slice(c * width, (c + 1) * width) for c in range(SPANS)]
    chunks = [(sub, span) for sub in range(subs) for span in spans]

    def rows_of_sub(sub):
        return slice(sub * SUB, (sub + 1) * SUB)

    def columns_of(which, span=slice(0, None)):
        start = span.start
        size = (half if span.stop is None else span.stop) - start
        return pl.ds(pl.multiple_of(which * half + start, size), size)

    own_mem = pl.ds(me * mem_dev, mem_dev)
    own_eig = pl.ds(core * modes_dev, modes_dev)

    loads = [
        (eig_all.at[:, own_eig], [
            (eig_hbm.at[:, rows_of_sub(sub), columns_of(core)], eig_all.at[sub, own_eig])
            for sub in range(subs)
        ]),
        (control, [(control_hbm, control)]),
        (cols, [(cols_hbm, cols)]),
        (owners, [(owners_hbm, owners)]),
        (all_ref.at[:, own_mem], [
            (mem_hbm.at[:, rows_of_sub(sub), columns_of(core)], all_ref.at[sub, own_mem])
            for sub in range(subs)
        ]),
        (interp, [(interp_hbm.at[:, :, own_obs], interp)]),
        (innov.at[tile], [
            (innov_hbm.at[0, pl.ds(tile * capacity, capacity), own_obs], innov.at[tile])
        ]),
        (obs.at[tile], [
            (obs_hbm.at[0, pl.ds(tile * capacity, capacity), own_obs], obs.at[tile])
        ]),
    ]

    def load(which):
        for i in which:
            for src, dst in loads[i][1]:
                pltpu.make_async_copy(src, dst, load_sem.at[i]).start()

    def loaded(which):
        for i in which:
            await_bytes(loads[i][0], load_sem.at[i])

    late = len(loads) - 3
    load(range(late))

    barrier = pltpu.get_barrier_semaphore()
    for step in range(1, nband):
        signal(barrier, "band", lax.rem(me + step, nband))
    place = snake(tile)
    heard = signal_beside(barrier, place, 1, tiles)
    pl.semaphore_wait(barrier, nband - 1 + heard)

    def send_members(c):
        sub, span = chunks[c]
        for far in range(1, chips):
            for step in range(CORES):
                target = lax.rem(core + step, CORES)
                peer = lax.rem(chip + far, chips) * CORES + target
                remote(
                    mem_hbm.at[:, rows_of_sub(sub), columns_of(target, span)],
                    all_ref.at[sub, own_mem, :, span], far_send, far_recv.at[c], band=peer,
                )

    for c in range(len(chunks)):
        send_members(c)
    for sub in range(subs):
        remote(
            eig_hbm.at[:, rows_of_sub(sub), columns_of(1 - core)], eig_all.at[sub, own_eig],
            eig_send, eig_recv.at[sub], band=partner,
        )
    for sub in range(subs):
        remote(
            mem_hbm.at[:, rows_of_sub(sub), columns_of(1 - core)], all_ref.at[sub, own_mem],
            mem_send, mem_recv.at[sub], band=partner,
        )
    load(range(late, len(loads)))
    heard = signal_beside(meet.at[0], place, 1, tiles)
    loaded(range(late))

    shape = (members * SUB, members)
    repeat = jnp.where(lax.div(iota(shape, 0), SUB) == iota(shape, 1), 1.0, 0.0).astype(BF16)
    rows_of = jnp.dot(repeat, control[...].astype(BF16), preferred_element_type=F32).astype(BF16)
    shape = (control.shape[1], modes_chip * SUB)
    widen = jnp.where(
        iota(shape, 0) == lax.div(iota(shape, 1), SUB) + chip * modes_chip, 1.0, 0.0
    ).astype(BF16)
    shape = (members * SUB, modes_chip * SUB)
    weight = jnp.where(
        lax.rem(iota(shape, 0), SUB) == lax.rem(iota(shape, 1), SUB),
        jnp.dot(rows_of, widen, preferred_element_type=F32), 0.0,
    ).astype(BF16)

    def meet_next(i, heard):
        pl.semaphore_wait(meet.at[i], heard)
        if i + 1 < rounds:
            return signal_beside(meet.at[i + 1], place, 1 << (i + 1), tiles)

    heard = meet_next(0, heard)

    def chip_sum(which, sub, span):
        rows = pl.ds(which * mem_chip, mem_chip)
        wide = all_ref[sub, rows, :, span].astype(F32)
        mem_wide[sub, rows, :, span] = wide
        return jnp.sum(wide * mixed[sub, rows, :, span], axis=0)

    for sub in range(subs):
        await_bytes(eig_all.at[sub, own_eig], eig_recv.at[sub])
        await_bytes(all_ref.at[sub, own_mem], mem_recv.at[sub])
        for span in spans:
            wide = eig_all[sub, :, :, span].astype(F32)
            eig_wide[sub, :, :, span] = wide
            mixed[sub, :, :, span] = jnp.dot(
                weight, wide.reshape(modes_chip * SUB, width).astype(BF16),
                preferred_element_type=F32,
            ).reshape(members, SUB, width)
            base[sub, :, span] = chip_sum(chip, sub, span)

    heard = meet_next(1, heard)
    column = iota((patch, half * CORES), 1)
    for j in range(blocks):
        select[j * patch : (j + 1) * patch] = jnp.where(
            cols[:, j : j + 1] == column, 1.0, 0.0
        ).astype(BF16)

    for i in range(2, rounds):
        heard = meet_next(i, heard)
    for step in range(1, tiles):
        peer = lax.rem(tile + step, tiles)
        rows = pl.ds(pl.multiple_of(peer * capacity, capacity), capacity)
        remote(
            innov_hbm.at[0, rows, own_obs], innov.at[tile], innov_send, innov_recv, mem=peer
        )
        remote(obs_hbm.at[0, rows, own_obs], obs.at[tile], obs_send, obs_recv, mem=peer)

    def finish(c):
        sub, span = chunks[c]
        await_bytes(all_ref.at[sub, : members - mem_chip, :, span], far_recv.at[c])
        total = base[sub, :, span]
        for far in range(1, chips):
            total = total + chip_sum(lax.rem(chip + far, chips), sub, span)
        parts[me, sub, :, span] = total
        for step in range(1, nband):
            block = parts.at[me, sub, :, span]
            remote(
                block, block, part_send, part_recv.at[c], band=lax.rem(me + step, nband)
            )

    def gather(c):
        sub, span = chunks[c]
        await_bytes(parts.at[: nband - 1, sub, :, span], part_recv.at[c])
        value = None
        for side in range(CORES):
            total = parts[side, sub, :, span]
            for other in range(1, chips):
                total = total + parts[other * CORES + side, sub, :, span]
            term = lax.dot_general(
                (scale * total).astype(BF16),
                select[:, side * half + span.start : side * half + span.stop],
                (((1,), (1,)), ((), ())), preferred_element_type=F32,
            )
            value = term if value is None else value + term
        if span.start == 0:
            spread[rows_of_sub(sub)] = value
        else:
            spread[rows_of_sub(sub)] += value

    per_group = DEPTH // patch
    groups = blocks // per_group
    diagonal = lax.div(iota((per_group, DEPTH), 1), patch) == iota((per_group, DEPTH), 0)

    def blocks_of(group, level):
        return jnp.concatenate([
            interp[
                group * per_group : (group + 1) * per_group, at * patch : (at + 1) * patch
            ].reshape(DEPTH, quarter)
            for at in (level, level + 1)
        ], axis=1)

    def project(sub):
        for group in range(groups):
            lanes = slice(group * DEPTH, (group + 1) * DEPTH)
            total = None
            for level in range(sub * SUB, (sub + 1) * SUB, 2):
                left = jnp.concatenate([
                    jnp.where(diagonal, spread[at : at + 1, lanes], 0.0)
                    for at in (level, level + 1)
                ], axis=0).astype(BF16)
                term = jnp.dot(left, blocks_of(group, level), preferred_element_type=F32)
                total = term if total is None else total + term
            value = total[:per_group, :quarter] + total[per_group:, quarter:]
            rows = slice(group * per_group, (group + 1) * per_group)
            if sub == 0:
                image[rows] = value
            else:
                image[rows] += value

    def spread_members(c):
        sub, span = chunks[c]
        for level in range(SUB):
            mem_lvl[sub * SUB + level, :, span] = mem_wide[sub, :, level, span]

    finish(0)
    for sub in range(subs):
        for level in range(SUB):
            eig_lvl[sub * SUB + level] = eig_wide[sub, :, level, :].astype(BF16)
    spread_members(0)

    for c in range(1, len(chunks) - 1):
        finish(c)
        spread_members(c)
    per_lane = owners.shape[1] // blocks
    line = owners[pl.ds(lax.div(tile, per_lane), 1)]
    owner = line[:, :blocks]
    for i in range(1, per_lane):
        owner = jnp.where(
            lax.rem(tile, per_lane) == i, line[:, i * blocks : (i + 1) * blocks], owner
        )
    owner = owner.astype(F32)
    down, across = iota((blocks, blocks), 0), iota((blocks, blocks), 1)
    owner_column = jnp.sum(jnp.where(down == across, owner, 0.0), axis=1, keepdims=True)
    same = jnp.where(jnp.logical_and(owner_column == owner, down < across), 1.0, 0.0)
    rank = jnp.sum(same, axis=0, keepdims=True)
    target = (owner * capacity + rank).astype(jnp.int32)
    placing = jnp.where(iota((tiles * capacity, blocks), 0) == target, 1.0, 0.0)
    loaded(range(late, len(loads)))
    others = slice(0, tiles - 1)
    await_bytes(innov.at[others], innov_recv)
    await_bytes(obs.at[others], obs_recv)

    def at_blocks(ref):
        return lax.dot_general(
            placing, ref[...].reshape(tiles * capacity, quarter), (((0,), (0,)), ((), ())),
            precision=HIGHEST, preferred_element_type=F32,
        )

    innov_block = at_blocks(innov)
    obs_block = at_blocks(obs)
    finish(len(chunks) - 1)
    for sub in range(subs):
        for c in range(sub * SPANS, (sub + 1) * SPANS):
            if c == len(chunks) - 1:
                spread_members(c)
            gather(c)
        project(sub)
    departure = obs_block * (innov_block - image[...])
    image[...] = departure

    rounded = departure.astype(BF16)
    blank = jnp.zeros((per_group, quarter), BF16)
    for group in range(groups):
        own = rounded[group * per_group : (group + 1) * per_group]
        left = jnp.concatenate([
            jnp.concatenate([own, blank], axis=1), jnp.concatenate([blank, own], axis=1)
        ], axis=0)
        for level in range(0, levels, 2):
            value = lax.dot_general(
                left, blocks_of(group, level), (((1,), (1,)), ((), ())),
                preferred_element_type=F32,
            )
            for k in range(2):
                upward[level + k : level + k + 1, group * DEPTH : (group + 1) * DEPTH] = jnp.sum(
                    jnp.where(diagonal, value[k * per_group : (k + 1) * per_group], 0.0),
                    axis=0, keepdims=True,
                )
    high = upward[...].astype(BF16)
    low = (upward[...] - high.astype(F32)).astype(BF16)
    left = jnp.concatenate([high, low], axis=0)
    far_peers = [lax.rem(chip + far, chips) * CORES for far in range(1, chips)]
    for c, span in enumerate(spans):
        value = jnp.dot(
            left,
            jnp.concatenate([
                select[:, columns_of(side, span)] for side in (1 - core, core)
            ], axis=1),
            preferred_element_type=F32,
        )
        value = value[:levels] + value[levels:]
        k = 0
        for own in range(CORES):
            side = core if own else 1 - core
            adj_out[own, :, span] = value[:, own * width : (own + 1) * width]
            peers = [peer + side for peer in far_peers]
            if not own:
                peers = [*peers, partner]
            for peer in peers:
                remote(
                    adj_out.at[own, :, span], adj_in.at[k, :, span],
                    adj_send, adj_recv.at[c], band=peer,
                )
                k += 1

    send[...] = jnp.dot(
        placing, image[...], precision=HIGHEST, preferred_element_type=F32
    ).reshape(send.shape)
    own_slots = pl.ds(pl.multiple_of(tile * capacity, capacity), capacity)
    for step in range(1, tiles):
        peer = lax.rem(tile + step, tiles)
        remote(send.at[peer], dep_ref.at[0, own_slots], dep_send, dep_recv, mem=peer)
    dep_ref[0, own_slots] = send[tile]
    local[...] = jnp.zeros_like(local)

    total = None
    for c, span in enumerate(spans):
        await_bytes(adj_in.at[:, :, span], adj_recv.at[c])
        adjoint = adj_out[1, :, span]
        for k in range(nband - 1):
            adjoint = adjoint + adj_in[k, :, span]
        for level in range(levels):
            weighted = (mem_lvl[level, :, span] * adjoint[level : level + 1]).astype(BF16)
            term = lax.dot_general(
                weighted, eig_lvl[level, :, span], (((1,), (1,)), ((), ())),
                preferred_element_type=F32,
            )
            total = term if total is None else total + term
    local[:, :modes_chip] = total
    rows = mem_dev // 2
    for b in range(nband):
        packed[b] = local[b * mem_dev : b * mem_dev + rows] + pltpu.roll(
            local[b * mem_dev + rows : (b + 1) * mem_dev], LANES // 2, 1
        )
    for far in range(tiles - 1, -1, -1):
        for step in range(nband - 1, -1, -1):
            if far or step:
                peer = lax.rem(me + step, nband)
                remote(
                    packed.at[peer], terms.at[me, tile], sum_send, sum_recv,
                    band=peer, mem=lax.rem(tile + far, tiles),
                )
    terms[me, tile] = packed[me]
    sums = terms.reshape(nband * tiles, rows, LANES)
    peers = nband * tiles - 1
    await_bytes(sums.at[:peers], sum_recv)
    whole = [jnp.zeros((rows, LANES), F32)] * 2
    lane = iota((rows, LANES), 1)
    for c in range(chips):
        value = terms[c * CORES, 0]
        for t in range(1, tiles * CORES):
            value = value + terms[c * CORES + t // tiles, t % tiles]
        for k in range(2):
            turned = value if k == 0 else pltpu.roll(value, LANES // 2, 1)
            turned = jnp.where(lane < modes_chip, turned, 0.0)
            whole[k] = whole[k] + (pltpu.roll(turned, c * modes_chip, 1) if c else turned)
    whole = jnp.concatenate(whole, axis=0)
    grad_ref[...] = (
        control[pl.ds(pl.multiple_of(me * mem_dev, mem_dev), mem_dev)]
        - scale * whole[:, : grad_ref.shape[1]]
    )
    await_bytes(dep_ref.at[0, : (tiles - 1) * capacity], dep_recv)
    sent = (
        (mem_hbm, far_send), (eig_all.at[:, own_eig], eig_send),
        (all_ref.at[:, own_mem], mem_send), (innov.at[others], innov_send),
        (obs.at[others], obs_send), (parts.at[: nband - 1], part_send), (adj_in, adj_send),
        (send.at[others], dep_send), (sums.at[:peers], sum_send),
    )
    for ref, semaphore in sent:
        for _ in range(chips - 1 if semaphore is far_send else 1):
            await_bytes(ref, semaphore)


def dma(*shape):
    return pltpu.SemaphoreType.DMA(shape)


def per_device(members, eigvecs, control, columns, interpolation, owners, innovation, obs_weight):
    nband = lax.axis_size("band")
    tiles = lax.axis_size("mem")
    mem_dev, levels, tile_cols = members.shape
    own_modes = eigvecs.shape[0]
    blocks, patch = columns.shape
    obs_block = interpolation.shape[2]
    capacity = innovation.shape[1] // tiles
    modes, total_members = control.shape
    scale = 1.0 / math.sqrt(modes * total_members)
    quarter = obs_block // nband
    half = tile_cols // CORES
    subs = levels // SUB
    chips = nband // CORES
    modes_chip = own_modes * CORES
    rounds = (tiles - 1).bit_length()
    slots = (tiles, capacity, quarter)
    own_slots = (1, tiles * capacity, quarter)
    owner_rows = owners.reshape(owners.shape[0] // LANES, LANES)
    hbm = pl.BlockSpec(memory_space=pltpu.HBM)
    vmem = pl.BlockSpec(memory_space=pltpu.VMEM)
    operands = (
        members, eigvecs, control.T, columns.T, interpolation, owner_rows, innovation, obs_weight
    )
    gradient, departure = pl.pallas_call(
        functools.partial(whole_kernel, nband, tiles, scale),
        out_shape=(
            jax.ShapeDtypeStruct((mem_dev, modes), F32),
            jax.ShapeDtypeStruct(own_slots, F32),
        ),
        in_specs=[hbm] * len(operands),
        out_specs=(vmem, vmem),
        scratch_shapes=[
            pltpu.VMEM((subs, total_members, SUB, half), BF16),
            pltpu.VMEM((subs, modes_chip, SUB, half), BF16),
            pltpu.VMEM((subs, modes_chip, SUB, half), F32),
            pltpu.VMEM((levels, modes_chip, half), BF16),
            pltpu.VMEM((total_members, modes), F32),
            pltpu.VMEM((patch, blocks), jnp.int32),
            pltpu.VMEM(owner_rows.shape, jnp.int32),
            pltpu.VMEM((subs, total_members, SUB, half), F32),
            pltpu.VMEM((subs, total_members, SUB, half), F32),
            pltpu.VMEM((levels, total_members, half), F32),
            pltpu.VMEM((subs, SUB, half), F32),
            pltpu.VMEM((nband, subs, SUB, half), F32),
            pltpu.VMEM((blocks * patch, tile_cols), BF16),
            pltpu.VMEM((blocks, levels * patch, quarter), BF16),
            pltpu.VMEM(slots, F32),
            pltpu.VMEM(slots, F32),
            pltpu.VMEM((levels, blocks * patch), F32),
            pltpu.VMEM((blocks, quarter), F32),
            pltpu.VMEM(slots, F32),
            pltpu.VMEM((levels, blocks * patch), F32),
            pltpu.VMEM((CORES, levels, half), F32),
            pltpu.VMEM((nband - 1, levels, half), F32),
            pltpu.VMEM((total_members, LANES), F32),
            pltpu.VMEM((nband, mem_dev // 2, LANES), F32),
            pltpu.VMEM((nband, tiles, mem_dev // 2, LANES), F32),
            pltpu.SemaphoreType.REGULAR((rounds,)),
            dma(8), dma(subs), dma(subs), dma(subs * SPANS), dma(subs * SPANS), dma(SPANS),
            *[dma() for _ in range(13)],
        ],
        compiler_params=pltpu.CompilerParams(
            collective_id=1, has_side_effects=True, vmem_limit_bytes=40 << 20
        ),
    )(*[pltpu.with_memory_space_constraint(x, pltpu.HBM) for x in operands])
    return (gradient.T, departure)


def solution(mesh):
    return jax.shard_map(
        per_device,
        mesh=mesh,
        in_specs=(
            P("band", None, "mem"),
            P("band", None, "mem"),
            P(),
            P("mem", None),
            P("mem", None, None),
            P(),
            P("mem", None, None),
            P("mem", None, None),
        ),
        out_specs=(P(None, "band"), P("mem", None, "band")),
        check_vma=False,
    )
```

```python
import functools
import math

import jax
import jax.numpy as jnp
from jax import lax
from jax.experimental import pallas as pl
from jax.experimental.pallas import tpu as pltpu
from jax.sharding import PartitionSpec as P

MESH = pl.DeviceIdType.MESH
CORES = 2
SUB = 8
DEPTH = 256
SPANS = 2
LANES = 128
F32, BF16 = jnp.float32, jnp.bfloat16
HIGHEST = lax.Precision.HIGHEST


def snake(index):
    row, column = lax.div(index, 2), lax.rem(index, 2)
    return index + lax.rem(row, 2) * (1 - 2 * column)


def signal(semaphore, axis, peer):
    pl.semaphore_signal(semaphore, inc=1, device_id={axis: peer}, device_id_type=MESH)


def signal_beside(semaphore, place, reach, size):
    def inform(there):
        @pl.when(jnp.logical_and(there >= 0, there < size))
        def _():
            signal(semaphore, "mem", snake(there))

    inform(place - reach)
    inform(place + reach)
    below = jnp.where(place >= reach, 1, 0)
    return below + jnp.where(place + reach < size, 1, 0)


def await_bytes(ref, semaphore):
    pltpu.make_async_copy(ref, ref, semaphore).wait()


def remote(src, dst, send, recv, **device):
    pltpu.make_async_remote_copy(
        src_ref=src, dst_ref=dst, send_sem=send, recv_sem=recv,
        device_id=device, device_id_type=MESH,
    ).start()


def iota(shape, dim):
    return lax.broadcasted_iota(jnp.int32, shape, dim)


def whole_kernel(
    nband, tiles, scale, mem_hbm, eig_hbm, control_hbm, cols_hbm, interp_hbm, owners_hbm,
    innov_hbm, obs_hbm, grad_ref, dep_ref,
    all_ref, eig_all, eig_wide, eig_lvl, control, cols, owners, mixed, mem_wide, mem_lvl,
    base, parts, select, interp, innov, obs, spread, image, send, upward, adj_out, adj_in,
    local, packed, terms, meet,
    load_sem, mem_recv, eig_recv, far_recv, part_recv, adj_recv,
    innov_recv, obs_recv, dep_recv, sum_recv,
    mem_send, eig_send, far_send, part_send, adj_send,
    innov_send, obs_send, dep_send, sum_send,
):
    me = lax.axis_index("band")
    tile = lax.axis_index("mem")
    chips = nband // CORES
    core = lax.rem(me, CORES)
    chip = lax.div(me, CORES)
    subs, members, _, half = all_ref.shape
    mem_dev = members // nband
    mem_chip = mem_dev * CORES
    modes_chip = eig_all.shape[1]
    modes_dev = modes_chip // CORES
    levels = subs * SUB
    patch, blocks = cols.shape
    capacity, quarter = send.shape[1:]
    rounds = meet.shape[0]
    partner = me + 1 - 2 * core
    own_obs = pl.ds(pl.multiple_of(me * quarter, quarter), quarter)
    width = half // SPANS
    spans = [slice(c * width, (c + 1) * width) for c in range(SPANS)]
    chunks = [(sub, span) for sub in range(subs) for span in spans]

    def rows_of_sub(sub):
        return slice(sub * SUB, (sub + 1) * SUB)

    def columns_of(which, span=slice(0, None)):
        start = span.start
        size = (half if span.stop is None else span.stop) - start
        return pl.ds(pl.multiple_of(which * half + start, size), size)

    own_mem = pl.ds(me * mem_dev, mem_dev)
    own_eig = pl.ds(core * modes_dev, modes_dev)

    loads = [
        (eig_all.at[:, own_eig], [
            (eig_hbm.at[:, rows_of_sub(sub), columns_of(core)], eig_all.at[sub, own_eig])
            for sub in range(subs)
        ]),
        (control, [(control_hbm, control)]),
        (cols, [(cols_hbm, cols)]),
        (owners, [(owners_hbm, owners)]),
        (all_ref.at[:, own_mem], [
            (mem_hbm.at[:, rows_of_sub(sub), columns_of(core)], all_ref.at[sub, own_mem])
            for sub in range(subs)
        ]),
        (interp, [(interp_hbm.at[:, :, own_obs], interp)]),
        (innov.at[tile], [
            (innov_hbm.at[0, pl.ds(tile * capacity, capacity), own_obs], innov.at[tile])
        ]),
        (obs.at[tile], [
            (obs_hbm.at[0, pl.ds(tile * capacity, capacity), own_obs], obs.at[tile])
        ]),
    ]

    def load(which):
        for i in which:
            for src, dst in loads[i][1]:
                pltpu.make_async_copy(src, dst, load_sem.at[i]).start()

    def loaded(which):
        for i in which:
            await_bytes(loads[i][0], load_sem.at[i])

    late = len(loads) - 3
    load(range(late))

    barrier = pltpu.get_barrier_semaphore()
    for step in range(1, nband):
        signal(barrier, "band", lax.rem(me + step, nband))
    place = snake(tile)
    heard = signal_beside(barrier, place, 1, tiles)
    pl.semaphore_wait(barrier, nband - 1 + heard)

    def send_members(c):
        sub, span = chunks[c]
        for far in range(1, chips):
            for step in range(CORES):
                target = lax.rem(core + step, CORES)
                peer = lax.rem(chip + far, chips) * CORES + target
                remote(
                    mem_hbm.at[:, rows_of_sub(sub), columns_of(target, span)],
                    all_ref.at[sub, own_mem, :, span], far_send, far_recv.at[c], band=peer,
                )

    for c in range(len(chunks)):
        send_members(c)
    for sub in range(subs):
        remote(
            eig_hbm.at[:, rows_of_sub(sub), columns_of(1 - core)], eig_all.at[sub, own_eig],
            eig_send, eig_recv.at[sub], band=partner,
        )
    for sub in range(subs):
        remote(
            mem_hbm.at[:, rows_of_sub(sub), columns_of(1 - core)], all_ref.at[sub, own_mem],
            mem_send, mem_recv.at[sub], band=partner,
        )
    load(range(late, len(loads)))
    heard = signal_beside(meet.at[0], place, 1, tiles)
    loaded(range(late))

    shape = (members * SUB, members)
    repeat = jnp.where(lax.div(iota(shape, 0), SUB) == iota(shape, 1), 1.0, 0.0).astype(BF16)
    rows_of = jnp.dot(repeat, control[...].astype(BF16), preferred_element_type=F32).astype(BF16)
    shape = (control.shape[1], modes_chip * SUB)
    widen = jnp.where(
        iota(shape, 0) == lax.div(iota(shape, 1), SUB) + chip * modes_chip, 1.0, 0.0
    ).astype(BF16)
    shape = (members * SUB, modes_chip * SUB)
    weight = jnp.where(
        lax.rem(iota(shape, 0), SUB) == lax.rem(iota(shape, 1), SUB),
        jnp.dot(rows_of, widen, preferred_element_type=F32), 0.0,
    ).astype(BF16)

    def meet_next(i, heard):
        pl.semaphore_wait(meet.at[i], heard)
        if i + 1 < rounds:
            return signal_beside(meet.at[i + 1], place, 1 << (i + 1), tiles)

    heard = meet_next(0, heard)

    def chip_sum(which, sub, span):
        rows = pl.ds(which * mem_chip, mem_chip)
        wide = all_ref[sub, rows, :, span].astype(F32)
        mem_wide[sub, rows, :, span] = wide
        return jnp.sum(wide * mixed[sub, rows, :, span], axis=0)

    for sub in range(subs):
        await_bytes(eig_all.at[sub, own_eig], eig_recv.at[sub])
        await_bytes(all_ref.at[sub, own_mem], mem_recv.at[sub])
        for span in spans:
            wide = eig_all[sub, :, :, span].astype(F32)
            eig_wide[sub, :, :, span] = wide
            mixed[sub, :, :, span] = jnp.dot(
                weight, wide.reshape(modes_chip * SUB, width).astype(BF16),
                preferred_element_type=F32,
            ).reshape(members, SUB, width)
            base[sub, :, span] = chip_sum(chip, sub, span)

    heard = meet_next(1, heard)
    column = iota((patch, half * CORES), 1)
    for j in range(blocks):
        select[j * patch : (j + 1) * patch] = jnp.where(
            cols[:, j : j + 1] == column, 1.0, 0.0
        ).astype(BF16)

    for i in range(2, rounds):
        heard = meet_next(i, heard)
    for step in range(1, tiles):
        peer = lax.rem(tile + step, tiles)
        rows = pl.ds(pl.multiple_of(peer * capacity, capacity), capacity)
        remote(
            innov_hbm.at[0, rows, own_obs], innov.at[tile], innov_send, innov_recv, mem=peer
        )
        remote(obs_hbm.at[0, rows, own_obs], obs.at[tile], obs_send, obs_recv, mem=peer)

    def finish(c):
        sub, span = chunks[c]
        await_bytes(all_ref.at[sub, : members - mem_chip, :, span], far_recv.at[c])
        total = base[sub, :, span]
        for far in range(1, chips):
            total = total + chip_sum(lax.rem(chip + far, chips), sub, span)
        parts[me, sub, :, span] = total
        for step in range(1, nband):
            block = parts.at[me, sub, :, span]
            remote(
                block, block, part_send, part_recv.at[c], band=lax.rem(me + step, nband)
            )

    def gather(c):
        sub, span = chunks[c]
        await_bytes(parts.at[: nband - 1, sub, :, span], part_recv.at[c])
        value = None
        for side in range(CORES):
            total = parts[side, sub, :, span]
            for other in range(1, chips):
                total = total + parts[other * CORES + side, sub, :, span]
            term = lax.dot_general(
                (scale * total).astype(BF16),
                select[:, side * half + span.start : side * half + span.stop],
                (((1,), (1,)), ((), ())), preferred_element_type=F32,
            )
            value = term if value is None else value + term
        if span.start == 0:
            spread[rows_of_sub(sub)] = value
        else:
            spread[rows_of_sub(sub)] += value

    per_group = DEPTH // patch
    groups = blocks // per_group
    diagonal = lax.div(iota((per_group, DEPTH), 1), patch) == iota((per_group, DEPTH), 0)

    def blocks_of(group, level):
        return jnp.concatenate([
            interp[
                group * per_group : (group + 1) * per_group, at * patch : (at + 1) * patch
            ].reshape(DEPTH, quarter)
            for at in (level, level + 1)
        ], axis=1)

    def project(sub):
        for group in range(groups):
            lanes = slice(group * DEPTH, (group + 1) * DEPTH)
            total = None
            for level in range(sub * SUB, (sub + 1) * SUB, 2):
                left = jnp.concatenate([
                    jnp.where(diagonal, spread[at : at + 1, lanes], 0.0)
                    for at in (level, level + 1)
                ], axis=0).astype(BF16)
                term = jnp.dot(left, blocks_of(group, level), preferred_element_type=F32)
                total = term if total is None else total + term
            value = total[:per_group, :quarter] + total[per_group:, quarter:]
            rows = slice(group * per_group, (group + 1) * per_group)
            if sub == 0:
                image[rows] = value
            else:
                image[rows] += value

    def spread_members(c):
        sub, span = chunks[c]
        for level in range(SUB):
            mem_lvl[sub * SUB + level, :, span] = mem_wide[sub, :, level, span]

    finish(0)
    for sub in range(subs):
        for level in range(SUB):
            eig_lvl[sub * SUB + level] = eig_wide[sub, :, level, :].astype(BF16)
    spread_members(0)

    for c in range(1, len(chunks) - 1):
        finish(c)
        spread_members(c)
    per_lane = owners.shape[1] // blocks
    line = owners[pl.ds(lax.div(tile, per_lane), 1)]
    owner = line[:, :blocks]
    for i in range(1, per_lane):
        owner = jnp.where(
            lax.rem(tile, per_lane) == i, line[:, i * blocks : (i + 1) * blocks], owner
        )
    owner = owner.astype(F32)
    down, across = iota((blocks, blocks), 0), iota((blocks, blocks), 1)
    owner_column = jnp.sum(jnp.where(down == across, owner, 0.0), axis=1, keepdims=True)
    same = jnp.where(jnp.logical_and(owner_column == owner, down < across), 1.0, 0.0)
    rank = jnp.sum(same, axis=0, keepdims=True)
    target = (owner * capacity + rank).astype(jnp.int32)
    placing = jnp.where(iota((tiles * capacity, blocks), 0) == target, 1.0, 0.0)
    others = slice(0, tiles - 1)

    def at_blocks(ref):
        return lax.dot_general(
            placing, ref[...].reshape(tiles * capacity, quarter), (((0,), (0,)), ((), ())),
            precision=HIGHEST, preferred_element_type=F32,
        )

    loaded([late])
    finish(len(chunks) - 1)
    for sub in range(subs):
        for c in range(sub * SPANS, (sub + 1) * SPANS):
            if c == len(chunks) - 1:
                spread_members(c)
                loaded(range(late + 1, len(loads)))
                await_bytes(innov.at[others], innov_recv)
                await_bytes(obs.at[others], obs_recv)
                innov_block = at_blocks(innov)
                obs_block = at_blocks(obs)
            gather(c)
        project(sub)
    departure = obs_block * (innov_block - image[...])
    image[...] = departure

    rounded = departure.astype(BF16)
    blank = jnp.zeros((per_group, quarter), BF16)
    for group in range(groups):
        own = rounded[group * per_group : (group + 1) * per_group]
        left = jnp.concatenate([
            jnp.concatenate([own, blank], axis=1), jnp.concatenate([blank, own], axis=1)
        ], axis=0)
        for level in range(0, levels, 2):
            value = lax.dot_general(
                left, blocks_of(group, level), (((1,), (1,)), ((), ())),
                preferred_element_type=F32,
            )
            for k in range(2):
                upward[level + k : level + k + 1, group * DEPTH : (group + 1) * DEPTH] = jnp.sum(
                    jnp.where(diagonal, value[k * per_group : (k + 1) * per_group], 0.0),
                    axis=0, keepdims=True,
                )
    high = upward[...].astype(BF16)
    low = (upward[...] - high.astype(F32)).astype(BF16)
    left = jnp.concatenate([high, low], axis=0)
    far_peers = [lax.rem(chip + far, chips) * CORES for far in range(1, chips)]
    for c, span in enumerate(spans):
        value = jnp.dot(
            left,
            jnp.concatenate([
                select[:, columns_of(side, span)] for side in (1 - core, core)
            ], axis=1),
            preferred_element_type=F32,
        )
        value = value[:levels] + value[levels:]
        k = 0
        for own in range(CORES):
            side = core if own else 1 - core
            adj_out[own, :, span] = value[:, own * width : (own + 1) * width]
            peers = [peer + side for peer in far_peers]
            if not own:
                peers = [*peers, partner]
            for peer in peers:
                remote(
                    adj_out.at[own, :, span], adj_in.at[k, :, span],
                    adj_send, adj_recv.at[c], band=peer,
                )
                k += 1

    send[...] = jnp.dot(
        placing, image[...], precision=HIGHEST, preferred_element_type=F32
    ).reshape(send.shape)
    own_slots = pl.ds(pl.multiple_of(tile * capacity, capacity), capacity)
    for step in range(1, tiles):
        peer = lax.rem(tile + step, tiles)
        remote(send.at[peer], dep_ref.at[0, own_slots], dep_send, dep_recv, mem=peer)
    dep_ref[0, own_slots] = send[tile]
    local[...] = jnp.zeros_like(local)

    total = None
    for c, span in enumerate(spans):
        await_bytes(adj_in.at[:, :, span], adj_recv.at[c])
        adjoint = adj_out[1, :, span]
        for k in range(nband - 1):
            adjoint = adjoint + adj_in[k, :, span]
        for level in range(levels):
            weighted = (mem_lvl[level, :, span] * adjoint[level : level + 1]).astype(BF16)
            term = lax.dot_general(
                weighted, eig_lvl[level, :, span], (((1,), (1,)), ((), ())),
                preferred_element_type=F32,
            )
            total = term if total is None else total + term
    local[:, :modes_chip] = total
    rows = mem_dev // 2
    for b in range(nband):
        packed[b] = local[b * mem_dev : b * mem_dev + rows] + pltpu.roll(
            local[b * mem_dev + rows : (b + 1) * mem_dev], LANES // 2, 1
        )
    for far in range(tiles - 1, -1, -1):
        for step in range(nband - 1, -1, -1):
            if far or step:
                peer = lax.rem(me + step, nband)
                remote(
                    packed.at[peer], terms.at[me, tile], sum_send, sum_recv,
                    band=peer, mem=lax.rem(tile + far, tiles),
                )
    terms[me, tile] = packed[me]
    sums = terms.reshape(nband * tiles, rows, LANES)
    peers = nband * tiles - 1
    await_bytes(sums.at[:peers], sum_recv)
    whole = [jnp.zeros((rows, LANES), F32)] * 2
    lane = iota((rows, LANES), 1)
    for c in range(chips):
        value = terms[c * CORES, 0]
        for t in range(1, tiles * CORES):
            value = value + terms[c * CORES + t // tiles, t % tiles]
        for k in range(2):
            turned = value if k == 0 else pltpu.roll(value, LANES // 2, 1)
            turned = jnp.where(lane < modes_chip, turned, 0.0)
            whole[k] = whole[k] + (pltpu.roll(turned, c * modes_chip, 1) if c else turned)
    whole = jnp.concatenate(whole, axis=0)
    grad_ref[...] = (
        control[pl.ds(pl.multiple_of(me * mem_dev, mem_dev), mem_dev)]
        - scale * whole[:, : grad_ref.shape[1]]
    )
    await_bytes(dep_ref.at[0, : (tiles - 1) * capacity], dep_recv)
    sent = (
        (mem_hbm, far_send), (eig_all.at[:, own_eig], eig_send),
        (all_ref.at[:, own_mem], mem_send), (innov.at[others], innov_send),
        (obs.at[others], obs_send), (parts.at[: nband - 1], part_send), (adj_in, adj_send),
        (send.at[others], dep_send), (sums.at[:peers], sum_send),
    )
    for ref, semaphore in sent:
        for _ in range(chips - 1 if semaphore is far_send else 1):
            await_bytes(ref, semaphore)


def write_out(grad_ref, dep_ref, grad_out, dep_out, sem):
    pairs = ((dep_ref, dep_out), (grad_ref, grad_out))
    copies = [pltpu.make_async_copy(*pair, sem.at[i]) for i, pair in enumerate(pairs)]
    for copy in copies:
        copy.start()
    for copy in copies:
        copy.wait()


def dma(*shape):
    return pltpu.SemaphoreType.DMA(shape)


def per_device(members, eigvecs, control, columns, interpolation, owners, innovation, obs_weight):
    nband = lax.axis_size("band")
    tiles = lax.axis_size("mem")
    mem_dev, levels, tile_cols = members.shape
    own_modes = eigvecs.shape[0]
    blocks, patch = columns.shape
    obs_block = interpolation.shape[2]
    capacity = innovation.shape[1] // tiles
    modes, total_members = control.shape
    scale = 1.0 / math.sqrt(modes * total_members)
    quarter = obs_block // nband
    half = tile_cols // CORES
    subs = levels // SUB
    chips = nband // CORES
    modes_chip = own_modes * CORES
    rounds = (tiles - 1).bit_length()
    slots = (tiles, capacity, quarter)
    own_slots = (1, tiles * capacity, quarter)
    owner_rows = owners.reshape(owners.shape[0] // LANES, LANES)
    hbm = pl.BlockSpec(memory_space=pltpu.HBM)
    vmem = pl.BlockSpec(memory_space=pltpu.VMEM)
    operands = (
        members, eigvecs, control.T, columns.T, interpolation, owner_rows, innovation, obs_weight
    )
    gradient, departure = pl.pallas_call(
        functools.partial(whole_kernel, nband, tiles, scale),
        out_shape=(
            jax.ShapeDtypeStruct((mem_dev, modes), F32),
            jax.ShapeDtypeStruct(own_slots, F32),
        ),
        in_specs=[hbm] * len(operands),
        out_specs=(vmem, vmem),
        scratch_shapes=[
            pltpu.VMEM((subs, total_members, SUB, half), BF16),
            pltpu.VMEM((subs, modes_chip, SUB, half), BF16),
            pltpu.VMEM((subs, modes_chip, SUB, half), F32),
            pltpu.VMEM((levels, modes_chip, half), BF16),
            pltpu.VMEM((total_members, modes), F32),
            pltpu.VMEM((patch, blocks), jnp.int32),
            pltpu.VMEM(owner_rows.shape, jnp.int32),
            pltpu.VMEM((subs, total_members, SUB, half), F32),
            pltpu.VMEM((subs, total_members, SUB, half), F32),
            pltpu.VMEM((levels, total_members, half), F32),
            pltpu.VMEM((subs, SUB, half), F32),
            pltpu.VMEM((nband, subs, SUB, half), F32),
            pltpu.VMEM((blocks * patch, tile_cols), BF16),
            pltpu.VMEM((blocks, levels * patch, quarter), BF16),
            pltpu.VMEM(slots, F32),
            pltpu.VMEM(slots, F32),
            pltpu.VMEM((levels, blocks * patch), F32),
            pltpu.VMEM((blocks, quarter), F32),
            pltpu.VMEM(slots, F32),
            pltpu.VMEM((levels, blocks * patch), F32),
            pltpu.VMEM((CORES, levels, half), F32),
            pltpu.VMEM((nband - 1, levels, half), F32),
            pltpu.VMEM((total_members, LANES), F32),
            pltpu.VMEM((nband, mem_dev // 2, LANES), F32),
            pltpu.VMEM((nband, tiles, mem_dev // 2, LANES), F32),
            pltpu.SemaphoreType.REGULAR((rounds,)),
            dma(8), dma(subs), dma(subs), dma(subs * SPANS), dma(subs * SPANS), dma(SPANS),
            *[dma() for _ in range(13)],
        ],
        compiler_params=pltpu.CompilerParams(
            collective_id=1, has_side_effects=True, vmem_limit_bytes=40 << 20
        ),
    )(*[pltpu.with_memory_space_constraint(x, pltpu.HBM) for x in operands])
    results = (gradient, departure)
    gradient, departure = pl.pallas_call(
        write_out,
        out_shape=tuple(jax.ShapeDtypeStruct(x.shape, x.dtype) for x in results),
        in_specs=[vmem, vmem],
        out_specs=(hbm, hbm),
        scratch_shapes=[dma(2)],
    )(*[pltpu.with_memory_space_constraint(x, pltpu.VMEM) for x in results])
    return (gradient.T, departure)


def solution(mesh):
    return jax.shard_map(
        per_device,
        mesh=mesh,
        in_specs=(
            P("band", None, "mem"),
            P("band", None, "mem"),
            P(),
            P("mem", None),
            P("mem", None, None),
            P(),
            P("mem", None, None),
            P("mem", None, None),
        ),
        out_specs=(P(None, "band"), P("mem", None, "band")),
        check_vma=False,
    )
```

```python
import functools
import math

import jax
import jax.numpy as jnp
from jax import lax
from jax.experimental import pallas as pl
from jax.experimental.pallas import tpu as pltpu
from jax.sharding import PartitionSpec as P

MESH = pl.DeviceIdType.MESH
CORES = 2
SUB = 8
DEPTH = 256
SPANS = 2
LANES = 128
F32, BF16 = jnp.float32, jnp.bfloat16
HIGHEST = lax.Precision.HIGHEST


def snake(index):
    row, column = lax.div(index, 2), lax.rem(index, 2)
    return index + lax.rem(row, 2) * (1 - 2 * column)


def signal(semaphore, axis, peer):
    pl.semaphore_signal(semaphore, inc=1, device_id={axis: peer}, device_id_type=MESH)


def signal_beside(semaphore, place, reach, size):
    def inform(there):
        @pl.when(jnp.logical_and(there >= 0, there < size))
        def _():
            signal(semaphore, "mem", snake(there))

    inform(place - reach)
    inform(place + reach)
    below = jnp.where(place >= reach, 1, 0)
    return below + jnp.where(place + reach < size, 1, 0)


def await_bytes(ref, semaphore):
    pltpu.make_async_copy(ref, ref, semaphore).wait()


def remote(src, dst, send, recv, **device):
    pltpu.make_async_remote_copy(
        src_ref=src, dst_ref=dst, send_sem=send, recv_sem=recv,
        device_id=device, device_id_type=MESH,
    ).start()


def iota(shape, dim):
    return lax.broadcasted_iota(jnp.int32, shape, dim)


def whole_kernel(
    nband, tiles, scale, mem_hbm, eig_hbm, control_hbm, cols_hbm, interp_hbm, owners_hbm,
    innov_hbm, obs_hbm, grad_ref, dep_ref,
    all_ref, eig_all, eig_wide, eig_lvl, control, cols, owners, mixed, mem_wide, mem_lvl,
    base, parts, select, interp, innov, obs, spread, image, send, upward, adj_out, adj_in,
    local, packed, terms, turned, meet,
    load_sem, mem_recv, eig_recv, far_recv, part_recv, adj_recv,
    innov_recv, obs_recv, dep_recv, sum_recv,
    mem_send, eig_send, far_send, part_send, adj_send,
    innov_send, obs_send, dep_send, sum_send,
):
    me = lax.axis_index("band")
    tile = lax.axis_index("mem")
    chips = nband // CORES
    core = lax.rem(me, CORES)
    chip = lax.div(me, CORES)
    subs, members, _, half = all_ref.shape
    mem_dev = members // nband
    mem_chip = mem_dev * CORES
    modes_chip = eig_all.shape[1]
    modes_dev = modes_chip // CORES
    levels = subs * SUB
    patch, blocks = cols.shape
    capacity, quarter = send.shape[1:]
    rounds = meet.shape[0]
    partner = me + 1 - 2 * core
    own_obs = pl.ds(pl.multiple_of(me * quarter, quarter), quarter)
    width = half // SPANS
    spans = [slice(c * width, (c + 1) * width) for c in range(SPANS)]
    chunks = [(sub, span) for sub in range(subs) for span in spans]

    def rows_of_sub(sub):
        return slice(sub * SUB, (sub + 1) * SUB)

    def columns_of(which, span=slice(0, None)):
        start = span.start
        size = (half if span.stop is None else span.stop) - start
        return pl.ds(pl.multiple_of(which * half + start, size), size)

    own_mem = pl.ds(me * mem_dev, mem_dev)
    own_eig = pl.ds(core * modes_dev, modes_dev)

    loads = [
        (eig_all.at[:, own_eig], [
            (eig_hbm.at[:, rows_of_sub(sub), columns_of(core)], eig_all.at[sub, own_eig])
            for sub in range(subs)
        ]),
        (control, [(control_hbm, control)]),
        (cols, [(cols_hbm, cols)]),
        (owners, [(owners_hbm, owners)]),
        (all_ref.at[:, own_mem], [
            (mem_hbm.at[:, rows_of_sub(sub), columns_of(core)], all_ref.at[sub, own_mem])
            for sub in range(subs)
        ]),
        (interp, [(interp_hbm.at[:, :, own_obs], interp)]),
        (innov.at[tile], [
            (innov_hbm.at[0, pl.ds(tile * capacity, capacity), own_obs], innov.at[tile])
        ]),
        (obs.at[tile], [
            (obs_hbm.at[0, pl.ds(tile * capacity, capacity), own_obs], obs.at[tile])
        ]),
    ]

    def load(which):
        for i in which:
            for src, dst in loads[i][1]:
                pltpu.make_async_copy(src, dst, load_sem.at[i]).start()

    def loaded(which):
        for i in which:
            await_bytes(loads[i][0], load_sem.at[i])

    late = len(loads) - 3
    load(range(late))

    barrier = pltpu.get_barrier_semaphore()
    for step in range(1, nband):
        signal(barrier, "band", lax.rem(me + step, nband))
    place = snake(tile)
    heard = signal_beside(barrier, place, 1, tiles)
    pl.semaphore_wait(barrier, nband - 1 + heard)

    def send_members(c):
        sub, span = chunks[c]
        for far in range(1, chips):
            for step in range(CORES):
                target = lax.rem(core + step, CORES)
                peer = lax.rem(chip + far, chips) * CORES + target
                remote(
                    mem_hbm.at[:, rows_of_sub(sub), columns_of(target, span)],
                    all_ref.at[sub, own_mem, :, span], far_send, far_recv.at[c], band=peer,
                )

    for c in range(len(chunks)):
        send_members(c)
    for sub in range(subs):
        remote(
            eig_hbm.at[:, rows_of_sub(sub), columns_of(1 - core)], eig_all.at[sub, own_eig],
            eig_send, eig_recv.at[sub], band=partner,
        )
    for sub in range(subs):
        remote(
            mem_hbm.at[:, rows_of_sub(sub), columns_of(1 - core)], all_ref.at[sub, own_mem],
            mem_send, mem_recv.at[sub], band=partner,
        )
    load(range(late, len(loads)))
    heard = signal_beside(meet.at[0], place, 1, tiles)
    loaded(range(late))

    shape = (members * SUB, members)
    repeat = jnp.where(lax.div(iota(shape, 0), SUB) == iota(shape, 1), 1.0, 0.0).astype(BF16)
    rows_of = jnp.dot(repeat, control[...].astype(BF16), preferred_element_type=F32).astype(BF16)
    shape = (control.shape[1], modes_chip * SUB)
    widen = jnp.where(
        iota(shape, 0) == lax.div(iota(shape, 1), SUB) + chip * modes_chip, 1.0, 0.0
    ).astype(BF16)
    shape = (members * SUB, modes_chip * SUB)
    weight = jnp.where(
        lax.rem(iota(shape, 0), SUB) == lax.rem(iota(shape, 1), SUB),
        jnp.dot(rows_of, widen, preferred_element_type=F32), 0.0,
    ).astype(BF16)

    def meet_next(i, heard):
        pl.semaphore_wait(meet.at[i], heard)
        if i + 1 < rounds:
            return signal_beside(meet.at[i + 1], place, 1 << (i + 1), tiles)

    heard = meet_next(0, heard)

    def chip_sum(which, sub, span):
        rows = pl.ds(which * mem_chip, mem_chip)
        wide = all_ref[sub, rows, :, span].astype(F32)
        mem_wide[sub, rows, :, span] = wide
        return jnp.sum(wide * mixed[sub, rows, :, span], axis=0)

    for sub in range(subs):
        await_bytes(eig_all.at[sub, own_eig], eig_recv.at[sub])
        await_bytes(all_ref.at[sub, own_mem], mem_recv.at[sub])
        for span in spans:
            wide = eig_all[sub, :, :, span].astype(F32)
            eig_wide[sub, :, :, span] = wide
            mixed[sub, :, :, span] = jnp.dot(
                weight, wide.reshape(modes_chip * SUB, width).astype(BF16),
                preferred_element_type=F32,
            ).reshape(members, SUB, width)
            base[sub, :, span] = chip_sum(chip, sub, span)

    heard = meet_next(1, heard)
    column = iota((patch, half * CORES), 1)
    for j in range(blocks):
        select[j * patch : (j + 1) * patch] = jnp.where(
            cols[:, j : j + 1] == column, 1.0, 0.0
        ).astype(BF16)

    for i in range(2, rounds):
        heard = meet_next(i, heard)
    for step in range(1, tiles):
        peer = lax.rem(tile + step, tiles)
        rows = pl.ds(pl.multiple_of(peer * capacity, capacity), capacity)
        remote(
            innov_hbm.at[0, rows, own_obs], innov.at[tile], innov_send, innov_recv, mem=peer
        )
        remote(obs_hbm.at[0, rows, own_obs], obs.at[tile], obs_send, obs_recv, mem=peer)

    def finish(c):
        sub, span = chunks[c]
        await_bytes(all_ref.at[sub, : members - mem_chip, :, span], far_recv.at[c])
        total = base[sub, :, span]
        for far in range(1, chips):
            total = total + chip_sum(lax.rem(chip + far, chips), sub, span)
        parts[me, sub, :, span] = total
        for step in range(1, nband):
            block = parts.at[me, sub, :, span]
            remote(
                block, block, part_send, part_recv.at[c], band=lax.rem(me + step, nband)
            )

    def gather(c):
        sub, span = chunks[c]
        await_bytes(parts.at[: nband - 1, sub, :, span], part_recv.at[c])
        value = None
        for side in range(CORES):
            total = parts[side, sub, :, span]
            for other in range(1, chips):
                total = total + parts[other * CORES + side, sub, :, span]
            term = lax.dot_general(
                (scale * total).astype(BF16),
                select[:, side * half + span.start : side * half + span.stop],
                (((1,), (1,)), ((), ())), preferred_element_type=F32,
            )
            value = term if value is None else value + term
        if span.start == 0:
            spread[rows_of_sub(sub)] = value
        else:
            spread[rows_of_sub(sub)] += value

    per_group = DEPTH // patch
    groups = blocks // per_group
    diagonal = lax.div(iota((per_group, DEPTH), 1), patch) == iota((per_group, DEPTH), 0)

    def blocks_of(group, level):
        return jnp.concatenate([
            interp[
                group * per_group : (group + 1) * per_group, at * patch : (at + 1) * patch
            ].reshape(DEPTH, quarter)
            for at in (level, level + 1)
        ], axis=1)

    def project(sub):
        for group in range(groups):
            lanes = slice(group * DEPTH, (group + 1) * DEPTH)
            total = None
            for level in range(sub * SUB, (sub + 1) * SUB, 2):
                left = jnp.concatenate([
                    jnp.where(diagonal, spread[at : at + 1, lanes], 0.0)
                    for at in (level, level + 1)
                ], axis=0).astype(BF16)
                term = jnp.dot(left, blocks_of(group, level), preferred_element_type=F32)
                total = term if total is None else total + term
            value = total[:per_group, :quarter] + total[per_group:, quarter:]
            rows = slice(group * per_group, (group + 1) * per_group)
            if sub == 0:
                image[rows] = value
            else:
                image[rows] += value

    def spread_members(c):
        sub, span = chunks[c]
        for level in range(SUB):
            mem_lvl[sub * SUB + level, :, span] = mem_wide[sub, :, level, span]

    eye = jnp.where(iota((DEPTH, DEPTH), 0) == iota((DEPTH, DEPTH), 1), 1.0, 0.0).astype(BF16)

    def turn_blocks(group):
        for level in range(0, levels, 2):
            turned[group, level // 2] = lax.dot_general(
                eye, blocks_of(group, level), (((1,), (1,)), ((), ())),
                preferred_element_type=F32,
            ).astype(BF16)

    finish(0)
    for sub in range(subs):
        for level in range(SUB):
            eig_lvl[sub * SUB + level] = eig_wide[sub, :, level, :].astype(BF16)
    spread_members(0)

    for c in range(1, len(chunks) - 1):
        finish(c)
        spread_members(c)
        if c == 1:
            loaded([late])
        share = pl.cdiv(groups, len(chunks) - 2)
        for group in range((c - 1) * share, min(c * share, groups)):
            turn_blocks(group)
    per_lane = owners.shape[1] // blocks
    line = owners[pl.ds(lax.div(tile, per_lane), 1)]
    owner = line[:, :blocks]
    for i in range(1, per_lane):
        owner = jnp.where(
            lax.rem(tile, per_lane) == i, line[:, i * blocks : (i + 1) * blocks], owner
        )
    owner = owner.astype(F32)
    down, across = iota((blocks, blocks), 0), iota((blocks, blocks), 1)
    owner_column = jnp.sum(jnp.where(down == across, owner, 0.0), axis=1, keepdims=True)
    same = jnp.where(jnp.logical_and(owner_column == owner, down < across), 1.0, 0.0)
    rank = jnp.sum(same, axis=0, keepdims=True)
    target = (owner * capacity + rank).astype(jnp.int32)
    placing = jnp.where(iota((tiles * capacity, blocks), 0) == target, 1.0, 0.0)
    others = slice(0, tiles - 1)

    finish(len(chunks) - 1)
    spread_members(len(chunks) - 1)
    for sub in range(subs):
        for c in range(sub * SPANS, (sub + 1) * SPANS):
            if c == len(chunks) - 1:
                loaded(range(late + 1, len(loads)))
                await_bytes(innov.at[others], innov_recv)
                await_bytes(obs.at[others], obs_recv)
                at_blocks = lax.dot_general(
                    placing, jnp.concatenate([
                        ref[...].reshape(tiles * capacity, quarter) for ref in (innov, obs)
                    ], axis=1), (((0,), (0,)), ((), ())),
                    precision=HIGHEST, preferred_element_type=F32,
                )
            gather(c)
        project(sub)
    departure = at_blocks[:, quarter:] * (at_blocks[:, :quarter] - image[...])
    image[...] = departure

    rounded = departure.astype(BF16)
    blank = jnp.zeros((per_group, quarter), BF16)
    for group in range(groups):
        own = rounded[group * per_group : (group + 1) * per_group]
        left = jnp.concatenate([
            jnp.concatenate([own, blank], axis=1), jnp.concatenate([blank, own], axis=1)
        ], axis=0)
        for level in range(0, levels, 2):
            value = jnp.dot(left, turned[group, level // 2], preferred_element_type=F32)
            for k in range(2):
                upward[level + k : level + k + 1, group * DEPTH : (group + 1) * DEPTH] = jnp.sum(
                    jnp.where(diagonal, value[k * per_group : (k + 1) * per_group], 0.0),
                    axis=0, keepdims=True,
                )
    high = upward[...].astype(BF16)
    low = (upward[...] - high.astype(F32)).astype(BF16)
    left = jnp.concatenate([high, low], axis=0)
    far_peers = [lax.rem(chip + far, chips) * CORES for far in range(1, chips)]
    for c, span in enumerate(spans):
        value = jnp.dot(
            left,
            jnp.concatenate([
                select[:, columns_of(side, span)] for side in (1 - core, core)
            ], axis=1),
            preferred_element_type=F32,
        )
        value = value[:levels] + value[levels:]
        k = 0
        for own in range(CORES):
            side = core if own else 1 - core
            adj_out[own, :, span] = value[:, own * width : (own + 1) * width]
            peers = [peer + side for peer in far_peers]
            if not own:
                peers = [*peers, partner]
            for peer in peers:
                remote(
                    adj_out.at[own, :, span], adj_in.at[k, :, span],
                    adj_send, adj_recv.at[c], band=peer,
                )
                k += 1

    send[...] = jnp.dot(
        placing, image[...], precision=HIGHEST, preferred_element_type=F32
    ).reshape(send.shape)
    own_slots = pl.ds(pl.multiple_of(tile * capacity, capacity), capacity)
    for step in range(1, tiles):
        peer = lax.rem(tile + step, tiles)
        remote(send.at[peer], dep_ref.at[0, own_slots], dep_send, dep_recv, mem=peer)
    dep_ref[0, own_slots] = send[tile]
    local[...] = jnp.zeros_like(local)

    total = None
    for c, span in enumerate(spans):
        await_bytes(adj_in.at[:, :, span], adj_recv.at[c])
        adjoint = adj_out[1, :, span]
        for k in range(nband - 1):
            adjoint = adjoint + adj_in[k, :, span]
        for level in range(levels):
            weighted = (mem_lvl[level, :, span] * adjoint[level : level + 1]).astype(BF16)
            term = lax.dot_general(
                weighted, eig_lvl[level, :, span], (((1,), (1,)), ((), ())),
                preferred_element_type=F32,
            )
            total = term if total is None else total + term
    local[:, :modes_chip] = total
    rows = mem_dev // 2
    for b in range(nband):
        packed[b] = local[b * mem_dev : b * mem_dev + rows] + pltpu.roll(
            local[b * mem_dev + rows : (b + 1) * mem_dev], LANES // 2, 1
        )
    for far in range(tiles - 1, -1, -1):
        for step in range(nband - 1, -1, -1):
            if far or step:
                peer = lax.rem(me + step, nband)
                remote(
                    packed.at[peer], terms.at[me, tile], sum_send, sum_recv,
                    band=peer, mem=lax.rem(tile + far, tiles),
                )
    terms[me, tile] = packed[me]
    sums = terms.reshape(nband * tiles, rows, LANES)
    peers = nband * tiles - 1
    await_bytes(sums.at[:peers], sum_recv)
    whole = [jnp.zeros((rows, LANES), F32)] * 2
    lane = iota((rows, LANES), 1)
    for c in range(chips):
        value = terms[c * CORES, 0]
        for t in range(1, tiles * CORES):
            value = value + terms[c * CORES + t // tiles, t % tiles]
        for k in range(2):
            moved = value if k == 0 else pltpu.roll(value, LANES // 2, 1)
            moved = jnp.where(lane < modes_chip, moved, 0.0)
            whole[k] = whole[k] + (pltpu.roll(moved, c * modes_chip, 1) if c else moved)
    whole = jnp.concatenate(whole, axis=0)
    grad_ref[...] = (
        control[pl.ds(pl.multiple_of(me * mem_dev, mem_dev), mem_dev)]
        - scale * whole[:, : grad_ref.shape[1]]
    )
    await_bytes(dep_ref.at[0, : (tiles - 1) * capacity], dep_recv)
    sent = (
        (mem_hbm, far_send), (eig_all.at[:, own_eig], eig_send),
        (all_ref.at[:, own_mem], mem_send), (innov.at[others], innov_send),
        (obs.at[others], obs_send), (parts.at[: nband - 1], part_send), (adj_in, adj_send),
        (send.at[others], dep_send), (sums.at[:peers], sum_send),
    )
    for ref, semaphore in sent:
        for _ in range(chips - 1 if semaphore is far_send else 1):
            await_bytes(ref, semaphore)


def write_out(grad_ref, dep_ref, grad_out, dep_out, sem):
    pairs = ((dep_ref, dep_out), (grad_ref, grad_out))
    copies = [pltpu.make_async_copy(*pair, sem.at[i]) for i, pair in enumerate(pairs)]
    for copy in copies:
        copy.start()
    for copy in copies:
        copy.wait()


def dma(*shape):
    return pltpu.SemaphoreType.DMA(shape)


def per_device(members, eigvecs, control, columns, interpolation, owners, innovation, obs_weight):
    nband = lax.axis_size("band")
    tiles = lax.axis_size("mem")
    mem_dev, levels, tile_cols = members.shape
    own_modes = eigvecs.shape[0]
    blocks, patch = columns.shape
    obs_block = interpolation.shape[2]
    capacity = innovation.shape[1] // tiles
    modes, total_members = control.shape
    scale = 1.0 / math.sqrt(modes * total_members)
    quarter = obs_block // nband
    half = tile_cols // CORES
    subs = levels // SUB
    chips = nband // CORES
    modes_chip = own_modes * CORES
    rounds = (tiles - 1).bit_length()
    slots = (tiles, capacity, quarter)
    own_slots = (1, tiles * capacity, quarter)
    owner_rows = owners.reshape(owners.shape[0] // LANES, LANES)
    hbm = pl.BlockSpec(memory_space=pltpu.HBM)
    vmem = pl.BlockSpec(memory_space=pltpu.VMEM)
    operands = (
        members, eigvecs, control.T, columns.T, interpolation, owner_rows, innovation, obs_weight
    )
    gradient, departure = pl.pallas_call(
        functools.partial(whole_kernel, nband, tiles, scale),
        out_shape=(
            jax.ShapeDtypeStruct((mem_dev, modes), F32),
            jax.ShapeDtypeStruct(own_slots, F32),
        ),
        in_specs=[hbm] * len(operands),
        out_specs=(vmem, vmem),
        scratch_shapes=[
            pltpu.VMEM((subs, total_members, SUB, half), BF16),
            pltpu.VMEM((subs, modes_chip, SUB, half), BF16),
            pltpu.VMEM((subs, modes_chip, SUB, half), F32),
            pltpu.VMEM((levels, modes_chip, half), BF16),
            pltpu.VMEM((total_members, modes), F32),
            pltpu.VMEM((patch, blocks), jnp.int32),
            pltpu.VMEM(owner_rows.shape, jnp.int32),
            pltpu.VMEM((subs, total_members, SUB, half), F32),
            pltpu.VMEM((subs, total_members, SUB, half), F32),
            pltpu.VMEM((levels, total_members, half), F32),
            pltpu.VMEM((subs, SUB, half), F32),
            pltpu.VMEM((nband, subs, SUB, half), F32),
            pltpu.VMEM((blocks * patch, tile_cols), BF16),
            pltpu.VMEM((blocks, levels * patch, quarter), BF16),
            pltpu.VMEM(slots, F32),
            pltpu.VMEM(slots, F32),
            pltpu.VMEM((levels, blocks * patch), F32),
            pltpu.VMEM((blocks, quarter), F32),
            pltpu.VMEM(slots, F32),
            pltpu.VMEM((levels, blocks * patch), F32),
            pltpu.VMEM((CORES, levels, half), F32),
            pltpu.VMEM((nband - 1, levels, half), F32),
            pltpu.VMEM((total_members, LANES), F32),
            pltpu.VMEM((nband, mem_dev // 2, LANES), F32),
            pltpu.VMEM((nband, tiles, mem_dev // 2, LANES), F32),
            pltpu.VMEM((blocks * patch // DEPTH, levels // 2, 2 * quarter, DEPTH), BF16),
            pltpu.SemaphoreType.REGULAR((rounds,)),
            dma(8), dma(subs), dma(subs), dma(subs * SPANS), dma(subs * SPANS), dma(SPANS),
            *[dma() for _ in range(13)],
        ],
        compiler_params=pltpu.CompilerParams(
            collective_id=1, has_side_effects=True, vmem_limit_bytes=40 << 20
        ),
    )(*[pltpu.with_memory_space_constraint(x, pltpu.HBM) for x in operands])
    results = (gradient, departure)
    gradient, departure = pl.pallas_call(
        write_out,
        out_shape=tuple(jax.ShapeDtypeStruct(x.shape, x.dtype) for x in results),
        in_specs=[vmem, vmem],
        out_specs=(hbm, hbm),
        scratch_shapes=[dma(2)],
    )(*[pltpu.with_memory_space_constraint(x, pltpu.VMEM) for x in results])
    return (gradient.T, departure)


def solution(mesh):
    return jax.shard_map(
        per_device,
        mesh=mesh,
        in_specs=(
            P("band", None, "mem"),
            P("band", None, "mem"),
            P(),
            P("mem", None),
            P("mem", None, None),
            P(),
            P("mem", None, None),
            P("mem", None, None),
        ),
        out_specs=(P(None, "band"), P("mem", None, "band")),
        check_vma=False,
    )
```

```python
import functools
import math

import jax
import jax.numpy as jnp
from jax import lax
from jax.experimental import pallas as pl
from jax.experimental.pallas import tpu as pltpu
from jax.sharding import PartitionSpec as P

MESH = pl.DeviceIdType.MESH
CORES = 2
SUB = 8
DEPTH = 256
SPANS = 2
LANES = 128
F32, BF16 = jnp.float32, jnp.bfloat16
HIGHEST = lax.Precision.HIGHEST


def snake(index):
    row, column = lax.div(index, 2), lax.rem(index, 2)
    return index + lax.rem(row, 2) * (1 - 2 * column)


def signal(semaphore, axis, peer):
    pl.semaphore_signal(semaphore, inc=1, device_id={axis: peer}, device_id_type=MESH)


def signal_beside(semaphore, place, reach, size):
    def inform(there):
        @pl.when(jnp.logical_and(there >= 0, there < size))
        def _():
            signal(semaphore, "mem", snake(there))

    inform(place - reach)
    inform(place + reach)
    below = jnp.where(place >= reach, 1, 0)
    return below + jnp.where(place + reach < size, 1, 0)


def await_bytes(ref, semaphore):
    pltpu.make_async_copy(ref, ref, semaphore).wait()


def remote(src, dst, send, recv, **device):
    pltpu.make_async_remote_copy(
        src_ref=src, dst_ref=dst, send_sem=send, recv_sem=recv,
        device_id=device, device_id_type=MESH,
    ).start()


def iota(shape, dim):
    return lax.broadcasted_iota(jnp.int32, shape, dim)


def whole_kernel(
    nband, tiles, scale, mem_hbm, eig_hbm, control_hbm, cols_hbm, interp_hbm, owners_hbm,
    innov_hbm, obs_hbm, grad_ref, dep_ref,
    all_ref, eig_all, eig_wide, eig_lvl, control, cols, owners, mixed, mem_wide, mem_lvl,
    base, parts, select, interp, innov, obs, spread, image, send, upward, adj_out, adj_in,
    local, packed, terms, turned, meet,
    load_sem, mem_recv, eig_recv, far_recv, part_recv, adj_recv,
    innov_recv, obs_recv, dep_recv, sum_recv,
    mem_send, eig_send, far_send, part_send, adj_send,
    innov_send, obs_send, dep_send, sum_send,
):
    me = lax.axis_index("band")
    tile = lax.axis_index("mem")
    chips = nband // CORES
    core = lax.rem(me, CORES)
    chip = lax.div(me, CORES)
    subs, members, _, half = all_ref.shape
    mem_dev = members // nband
    mem_chip = mem_dev * CORES
    modes_chip = eig_all.shape[1]
    modes_dev = modes_chip // CORES
    levels = subs * SUB
    patch, blocks = cols.shape
    capacity, quarter = send.shape[1:]
    rounds = meet.shape[0]
    partner = me + 1 - 2 * core
    own_obs = pl.ds(pl.multiple_of(me * quarter, quarter), quarter)
    width = half // SPANS
    spans = [slice(c * width, (c + 1) * width) for c in range(SPANS)]
    chunks = [(sub, span) for sub in range(subs) for span in spans]

    def rows_of_sub(sub):
        return slice(sub * SUB, (sub + 1) * SUB)

    def columns_of(which, span=slice(0, None)):
        start = span.start
        size = (half if span.stop is None else span.stop) - start
        return pl.ds(pl.multiple_of(which * half + start, size), size)

    own_mem = pl.ds(me * mem_dev, mem_dev)
    own_eig = pl.ds(core * modes_dev, modes_dev)

    loads = [
        (eig_all.at[:, own_eig], [
            (eig_hbm.at[:, rows_of_sub(sub), columns_of(core)], eig_all.at[sub, own_eig])
            for sub in range(subs)
        ]),
        (control, [(control_hbm, control)]),
        (cols, [(cols_hbm, cols)]),
        (owners, [(owners_hbm, owners)]),
        (all_ref.at[:, own_mem], [
            (mem_hbm.at[:, rows_of_sub(sub), columns_of(core)], all_ref.at[sub, own_mem])
            for sub in range(subs)
        ]),
        (interp, [(interp_hbm.at[:, :, own_obs], interp)]),
        (innov.at[tile], [
            (innov_hbm.at[0, pl.ds(tile * capacity, capacity), own_obs], innov.at[tile])
        ]),
        (obs.at[tile], [
            (obs_hbm.at[0, pl.ds(tile * capacity, capacity), own_obs], obs.at[tile])
        ]),
    ]

    def load(which):
        for i in which:
            for src, dst in loads[i][1]:
                pltpu.make_async_copy(src, dst, load_sem.at[i]).start()

    def loaded(which):
        for i in which:
            await_bytes(loads[i][0], load_sem.at[i])

    late = len(loads) - 3
    load(range(late))

    barrier = pltpu.get_barrier_semaphore()
    for step in range(1, nband):
        signal(barrier, "band", lax.rem(me + step, nband))
    place = snake(tile)
    heard = signal_beside(barrier, place, 1, tiles)
    pl.semaphore_wait(barrier, nband - 1 + heard)

    def send_members(c):
        sub, span = chunks[c]
        for far in range(1, chips):
            for step in range(CORES):
                target = lax.rem(core + step, CORES)
                peer = lax.rem(chip + far, chips) * CORES + target
                remote(
                    mem_hbm.at[:, rows_of_sub(sub), columns_of(target, span)],
                    all_ref.at[sub, own_mem, :, span], far_send, far_recv.at[c], band=peer,
                )

    for c in range(len(chunks)):
        send_members(c)
    for sub in range(subs):
        remote(
            eig_hbm.at[:, rows_of_sub(sub), columns_of(1 - core)], eig_all.at[sub, own_eig],
            eig_send, eig_recv.at[sub], band=partner,
        )
    for sub in range(subs):
        remote(
            mem_hbm.at[:, rows_of_sub(sub), columns_of(1 - core)], all_ref.at[sub, own_mem],
            mem_send, mem_recv.at[sub], band=partner,
        )
    load(range(late, len(loads)))
    heard = signal_beside(meet.at[0], place, 1, tiles)
    loaded(range(late))

    shape = (members * SUB, members)
    repeat = jnp.where(lax.div(iota(shape, 0), SUB) == iota(shape, 1), 1.0, 0.0).astype(BF16)
    rows_of = jnp.dot(repeat, control[...].astype(BF16), preferred_element_type=F32).astype(BF16)
    shape = (control.shape[1], modes_chip * SUB)
    widen = jnp.where(
        iota(shape, 0) == lax.div(iota(shape, 1), SUB) + chip * modes_chip, 1.0, 0.0
    ).astype(BF16)
    shape = (members * SUB, modes_chip * SUB)
    weight = jnp.where(
        lax.rem(iota(shape, 0), SUB) == lax.rem(iota(shape, 1), SUB),
        jnp.dot(rows_of, widen, preferred_element_type=F32), 0.0,
    ).astype(BF16)

    def meet_next(i, heard):
        pl.semaphore_wait(meet.at[i], heard)
        if i + 1 < rounds:
            return signal_beside(meet.at[i + 1], place, 1 << (i + 1), tiles)

    heard = meet_next(0, heard)

    def chip_sum(which, sub, span):
        rows = pl.ds(which * mem_chip, mem_chip)
        wide = all_ref[sub, rows, :, span].astype(F32)
        mem_wide[sub, rows, :, span] = wide
        return jnp.sum(wide * mixed[sub, rows, :, span], axis=0)

    for sub in range(subs):
        await_bytes(eig_all.at[sub, own_eig], eig_recv.at[sub])
        await_bytes(all_ref.at[sub, own_mem], mem_recv.at[sub])
        for span in spans:
            wide = eig_all[sub, :, :, span].astype(F32)
            eig_wide[sub, :, :, span] = wide
            mixed[sub, :, :, span] = jnp.dot(
                weight, wide.reshape(modes_chip * SUB, width).astype(BF16),
                preferred_element_type=F32,
            ).reshape(members, SUB, width)
            base[sub, :, span] = chip_sum(chip, sub, span)

    heard = meet_next(1, heard)
    column = iota((patch, half * CORES), 1)
    for j in range(blocks):
        select[j * patch : (j + 1) * patch] = jnp.where(
            cols[:, j : j + 1] == column, 1.0, 0.0
        ).astype(BF16)

    for i in range(2, rounds):
        heard = meet_next(i, heard)
    for step in range(1, tiles):
        peer = lax.rem(tile + step, tiles)
        rows = pl.ds(pl.multiple_of(peer * capacity, capacity), capacity)
        remote(
            innov_hbm.at[0, rows, own_obs], innov.at[tile], innov_send, innov_recv, mem=peer
        )
        remote(obs_hbm.at[0, rows, own_obs], obs.at[tile], obs_send, obs_recv, mem=peer)

    def finish(c):
        sub, span = chunks[c]
        await_bytes(all_ref.at[sub, : members - mem_chip, :, span], far_recv.at[c])
        total = base[sub, :, span]
        for far in range(1, chips):
            total = total + chip_sum(lax.rem(chip + far, chips), sub, span)
        parts[me, sub, :, span] = total
        for step in range(1, nband):
            block = parts.at[me, sub, :, span]
            remote(
                block, block, part_send, part_recv.at[c], band=lax.rem(me + step, nband)
            )

    def gather(c):
        sub, span = chunks[c]
        await_bytes(parts.at[: nband - 1, sub, :, span], part_recv.at[c])
        value = None
        for side in range(CORES):
            total = parts[side, sub, :, span]
            for other in range(1, chips):
                total = total + parts[other * CORES + side, sub, :, span]
            term = lax.dot_general(
                (scale * total).astype(BF16),
                select[:, side * half + span.start : side * half + span.stop],
                (((1,), (1,)), ((), ())), preferred_element_type=F32,
            )
            value = term if value is None else value + term
        if span.start == 0:
            spread[rows_of_sub(sub)] = value
        else:
            spread[rows_of_sub(sub)] += value

    per_group = DEPTH // patch
    groups = blocks // per_group
    diagonal = lax.div(iota((per_group, DEPTH), 1), patch) == iota((per_group, DEPTH), 0)

    def blocks_of(group, level):
        return jnp.concatenate([
            interp[
                group * per_group : (group + 1) * per_group, at * patch : (at + 1) * patch
            ].reshape(DEPTH, quarter)
            for at in (level, level + 1)
        ], axis=1)

    def project(sub):
        for group in range(groups):
            lanes = slice(group * DEPTH, (group + 1) * DEPTH)
            total = None
            for level in range(sub * SUB, (sub + 1) * SUB, 2):
                left = jnp.concatenate([
                    jnp.where(diagonal, spread[at : at + 1, lanes], 0.0)
                    for at in (level, level + 1)
                ], axis=0).astype(BF16)
                term = jnp.dot(left, blocks_of(group, level), preferred_element_type=F32)
                total = term if total is None else total + term
            value = total[:per_group, :quarter] + total[per_group:, quarter:]
            rows = slice(group * per_group, (group + 1) * per_group)
            if sub == 0:
                image[rows] = value
            else:
                image[rows] += value

    def spread_members(c):
        sub, span = chunks[c]
        for level in range(SUB):
            mem_lvl[sub * SUB + level, :, span] = mem_wide[sub, :, level, span]

    eye = jnp.where(iota((DEPTH, DEPTH), 0) == iota((DEPTH, DEPTH), 1), 1.0, 0.0).astype(BF16)

    def turn_blocks(group):
        for level in range(0, levels, 2):
            turned[group, level // 2] = lax.dot_general(
                eye, blocks_of(group, level), (((1,), (1,)), ((), ())),
                preferred_element_type=F32,
            ).astype(BF16)

    finish(0)
    for sub in range(subs):
        for level in range(SUB):
            eig_lvl[sub * SUB + level] = eig_wide[sub, :, level, :].astype(BF16)
    spread_members(0)

    for c in range(1, len(chunks) - 1):
        finish(c)
        spread_members(c)
        if c == 1:
            loaded([late])
        share = pl.cdiv(groups, len(chunks) - 2)
        for group in range((c - 1) * share, min(c * share, groups)):
            turn_blocks(group)
    per_lane = owners.shape[1] // blocks
    line = owners[pl.ds(lax.div(tile, per_lane), 1)]
    owner = line[:, :blocks]
    for i in range(1, per_lane):
        owner = jnp.where(
            lax.rem(tile, per_lane) == i, line[:, i * blocks : (i + 1) * blocks], owner
        )
    owner = owner.astype(F32)
    down, across = iota((blocks, blocks), 0), iota((blocks, blocks), 1)
    owner_column = jnp.sum(jnp.where(down == across, owner, 0.0), axis=1, keepdims=True)
    same = jnp.where(jnp.logical_and(owner_column == owner, down < across), 1.0, 0.0)
    rank = jnp.sum(same, axis=0, keepdims=True)
    target = (owner * capacity + rank).astype(jnp.int32)
    placing = jnp.where(iota((tiles * capacity, blocks), 0) == target, 1.0, 0.0)
    others = slice(0, tiles - 1)

    finish(len(chunks) - 1)
    spread_members(len(chunks) - 1)
    for sub in range(subs):
        for c in range(sub * SPANS, (sub + 1) * SPANS):
            if c == len(chunks) - 1:
                loaded(range(late + 1, len(loads)))
                await_bytes(innov.at[others], innov_recv)
                await_bytes(obs.at[others], obs_recv)
                at_blocks = lax.dot_general(
                    placing, jnp.concatenate([
                        ref[...].reshape(tiles * capacity, quarter) for ref in (innov, obs)
                    ], axis=1), (((0,), (0,)), ((), ())),
                    precision=HIGHEST, preferred_element_type=F32,
                )
            gather(c)
        project(sub)
    departure = at_blocks[:, quarter:] * (at_blocks[:, :quarter] - image[...])
    image[...] = departure

    rounded = departure.astype(BF16)
    blank = jnp.zeros((per_group, quarter), BF16)
    for group in range(groups):
        own = rounded[group * per_group : (group + 1) * per_group]
        left = jnp.concatenate([
            jnp.concatenate([own, blank], axis=1), jnp.concatenate([blank, own], axis=1)
        ], axis=0)
        for level in range(0, levels, 2):
            value = jnp.dot(left, turned[group, level // 2], preferred_element_type=F32)
            for k in range(2):
                upward[level + k : level + k + 1, group * DEPTH : (group + 1) * DEPTH] = jnp.sum(
                    jnp.where(diagonal, value[k * per_group : (k + 1) * per_group], 0.0),
                    axis=0, keepdims=True,
                )
    high = upward[...].astype(BF16)
    low = (upward[...] - high.astype(F32)).astype(BF16)
    left = jnp.concatenate([high, low], axis=0)
    far_peers = [lax.rem(chip + far, chips) * CORES for far in range(1, chips)]
    for c, span in enumerate(spans):
        value = jnp.dot(
            left,
            jnp.concatenate([
                select[:, columns_of(side, span)] for side in (1 - core, core)
            ], axis=1),
            preferred_element_type=F32,
        )
        value = value[:levels] + value[levels:]
        k = 0
        for own in range(CORES):
            side = core if own else 1 - core
            adj_out[own, :, span] = value[:, own * width : (own + 1) * width]
            peers = [peer + side for peer in far_peers]
            if not own:
                peers = [*peers, partner]
            for peer in peers:
                remote(
                    adj_out.at[own, :, span], adj_in.at[k, :, span],
                    adj_send, adj_recv.at[c], band=peer,
                )
                k += 1

    send[...] = jnp.dot(
        placing, image[...], precision=HIGHEST, preferred_element_type=F32
    ).reshape(send.shape)
    own_slots = pl.ds(pl.multiple_of(tile * capacity, capacity), capacity)
    for step in range(1, tiles):
        peer = lax.rem(tile + step, tiles)
        remote(send.at[peer], dep_ref.at[0, own_slots], dep_send, dep_recv, mem=peer)
    dep_ref[0, own_slots] = send[tile]
    local[...] = jnp.zeros_like(local)

    total = None
    for c, span in enumerate(spans):
        await_bytes(adj_in.at[:, :, span], adj_recv.at[c])
        adjoint = adj_out[1, :, span]
        for k in range(nband - 1):
            adjoint = adjoint + adj_in[k, :, span]
        for level in range(levels):
            weighted = (mem_lvl[level, :, span] * adjoint[level : level + 1]).astype(BF16)
            term = lax.dot_general(
                weighted, eig_lvl[level, :, span], (((1,), (1,)), ((), ())),
                preferred_element_type=F32,
            )
            total = term if total is None else total + term
    local[:, :modes_chip] = total
    rows = mem_dev // 2
    for b in range(nband):
        packed[b] = (local[b * mem_dev : b * mem_dev + rows] + pltpu.roll(
            local[b * mem_dev + rows : (b + 1) * mem_dev], LANES // 2, 1
        )).astype(BF16)
    for far in range(tiles - 1, -1, -1):
        for step in range(nband - 1, -1, -1):
            if far or step:
                peer = lax.rem(me + step, nband)
                remote(
                    packed.at[peer], terms.at[me, tile], sum_send, sum_recv,
                    band=peer, mem=lax.rem(tile + far, tiles),
                )
    terms[me, tile] = packed[me]
    sums = terms.reshape(nband * tiles, rows, LANES)
    peers = nband * tiles - 1
    await_bytes(sums.at[:peers], sum_recv)
    whole = [jnp.zeros((rows, LANES), F32)] * 2
    lane = iota((rows, LANES), 1)
    for c in range(chips):
        value = terms[c * CORES, 0].astype(F32)
        for t in range(1, tiles * CORES):
            value = value + terms[c * CORES + t // tiles, t % tiles].astype(F32)
        for k in range(2):
            moved = value if k == 0 else pltpu.roll(value, LANES // 2, 1)
            moved = jnp.where(lane < modes_chip, moved, 0.0)
            whole[k] = whole[k] + (pltpu.roll(moved, c * modes_chip, 1) if c else moved)
    whole = jnp.concatenate(whole, axis=0)
    grad_ref[...] = (
        control[pl.ds(pl.multiple_of(me * mem_dev, mem_dev), mem_dev)]
        - scale * whole[:, : grad_ref.shape[1]]
    )
    await_bytes(dep_ref.at[0, : (tiles - 1) * capacity], dep_recv)
    sent = (
        (mem_hbm, far_send), (eig_all.at[:, own_eig], eig_send),
        (all_ref.at[:, own_mem], mem_send), (innov.at[others], innov_send),
        (obs.at[others], obs_send), (parts.at[: nband - 1], part_send), (adj_in, adj_send),
        (send.at[others], dep_send), (sums.at[:peers], sum_send),
    )
    for ref, semaphore in sent:
        for _ in range(chips - 1 if semaphore is far_send else 1):
            await_bytes(ref, semaphore)


def write_out(grad_ref, dep_ref, grad_out, dep_out, sem):
    pairs = ((dep_ref, dep_out), (grad_ref, grad_out))
    copies = [pltpu.make_async_copy(*pair, sem.at[i]) for i, pair in enumerate(pairs)]
    for copy in copies:
        copy.start()
    for copy in copies:
        copy.wait()


def dma(*shape):
    return pltpu.SemaphoreType.DMA(shape)


def per_device(members, eigvecs, control, columns, interpolation, owners, innovation, obs_weight):
    nband = lax.axis_size("band")
    tiles = lax.axis_size("mem")
    mem_dev, levels, tile_cols = members.shape
    own_modes = eigvecs.shape[0]
    blocks, patch = columns.shape
    obs_block = interpolation.shape[2]
    capacity = innovation.shape[1] // tiles
    modes, total_members = control.shape
    scale = 1.0 / math.sqrt(modes * total_members)
    quarter = obs_block // nband
    half = tile_cols // CORES
    subs = levels // SUB
    chips = nband // CORES
    modes_chip = own_modes * CORES
    rounds = (tiles - 1).bit_length()
    slots = (tiles, capacity, quarter)
    own_slots = (1, tiles * capacity, quarter)
    owner_rows = owners.reshape(owners.shape[0] // LANES, LANES)
    hbm = pl.BlockSpec(memory_space=pltpu.HBM)
    vmem = pl.BlockSpec(memory_space=pltpu.VMEM)
    operands = (
        members, eigvecs, control.T, columns.T, interpolation, owner_rows, innovation, obs_weight
    )
    gradient, departure = pl.pallas_call(
        functools.partial(whole_kernel, nband, tiles, scale),
        out_shape=(
            jax.ShapeDtypeStruct((mem_dev, modes), F32),
            jax.ShapeDtypeStruct(own_slots, F32),
        ),
        in_specs=[hbm] * len(operands),
        out_specs=(vmem, vmem),
        scratch_shapes=[
            pltpu.VMEM((subs, total_members, SUB, half), BF16),
            pltpu.VMEM((subs, modes_chip, SUB, half), BF16),
            pltpu.VMEM((subs, modes_chip, SUB, half), F32),
            pltpu.VMEM((levels, modes_chip, half), BF16),
            pltpu.VMEM((total_members, modes), F32),
            pltpu.VMEM((patch, blocks), jnp.int32),
            pltpu.VMEM(owner_rows.shape, jnp.int32),
            pltpu.VMEM((subs, total_members, SUB, half), F32),
            pltpu.VMEM((subs, total_members, SUB, half), F32),
            pltpu.VMEM((levels, total_members, half), F32),
            pltpu.VMEM((subs, SUB, half), F32),
            pltpu.VMEM((nband, subs, SUB, half), F32),
            pltpu.VMEM((blocks * patch, tile_cols), BF16),
            pltpu.VMEM((blocks, levels * patch, quarter), BF16),
            pltpu.VMEM(slots, F32),
            pltpu.VMEM(slots, F32),
            pltpu.VMEM((levels, blocks * patch), F32),
            pltpu.VMEM((blocks, quarter), F32),
            pltpu.VMEM(slots, F32),
            pltpu.VMEM((levels, blocks * patch), F32),
            pltpu.VMEM((CORES, levels, half), F32),
            pltpu.VMEM((nband - 1, levels, half), F32),
            pltpu.VMEM((total_members, LANES), F32),
            pltpu.VMEM((nband, mem_dev // 2, LANES), BF16),
            pltpu.VMEM((nband, tiles, mem_dev // 2, LANES), BF16),
            pltpu.VMEM((blocks * patch // DEPTH, levels // 2, 2 * quarter, DEPTH), BF16),
            pltpu.SemaphoreType.REGULAR((rounds,)),
            dma(8), dma(subs), dma(subs), dma(subs * SPANS), dma(subs * SPANS), dma(SPANS),
            *[dma() for _ in range(13)],
        ],
        compiler_params=pltpu.CompilerParams(
            collective_id=1, has_side_effects=True, vmem_limit_bytes=40 << 20
        ),
    )(*[pltpu.with_memory_space_constraint(x, pltpu.HBM) for x in operands])
    results = (gradient, departure)
    gradient, departure = pl.pallas_call(
        write_out,
        out_shape=tuple(jax.ShapeDtypeStruct(x.shape, x.dtype) for x in results),
        in_specs=[vmem, vmem],
        out_specs=(hbm, hbm),
        scratch_shapes=[dma(2)],
    )(*[pltpu.with_memory_space_constraint(x, pltpu.VMEM) for x in results])
    return (gradient.T, departure)


def solution(mesh):
    return jax.shard_map(
        per_device,
        mesh=mesh,
        in_specs=(
            P("band", None, "mem"),
            P("band", None, "mem"),
            P(),
            P("mem", None),
            P("mem", None, None),
            P(),
            P("mem", None, None),
            P("mem", None, None),
        ),
        out_specs=(P(None, "band"), P("mem", None, "band")),
        check_vma=False,
    )
```
